128 devices in a mesh: seq: 16 (over x, y_hi, core), filt: 8 (over y_lo, z).
Axes of the slice: x: 4, y: 4 (y_hi: 2, y_lo: 2; y = y_hi * 2 + y_lo), z: 4, core: 2. Of those that a mesh axis runs over, the one named last changes fastest.
Arguments:
- tokens: bfloat16 [43008, 1024], P('seq', 'filt'), may hold values from -6 to 6
- conv_weight: bfloat16 [2, 3, 1024, 1024], P(None, None, None, 'filt'), may hold values from -0.109375 to 0.109375
- conv_bias: float32 [2, 1024], P(None, 'filt'), may hold values from -3 to 3
- mix_weight: bfloat16 [2, 1024, 1024], P(None, None, 'filt'), may hold values from -0.1875 to 0.1875
- mix_bias: float32 [2, 1024], P(None, 'filt'), may hold values from -3 to 3
- norm_gain: float32 [2, 1024], replicated, may hold values from 0.1 to 1.9
Outputs:
- layer_output: bfloat16 [43008, 1024], P('seq', 'filt')
The draws below stay inside these ranges and needn't reach their ends.
All inputs are finite; a program needn't handle non-finite values.
Results may differ from the reference program's by a relative error of at most 0.014.
Values may be sent and summed in bfloat16 or wider, within the bound.
No kernel may reach another device: no remote copies, remote signals or barrier semaphores. Data moves between devices by JAX's collectives and lax.ppermute only.
A program may use at most 64 MiB of HBM per device.

```python
import jax
import jax.numpy as jnp
from jax import lax

C = 1024
LAYERS = 2
POS_DEV = 2688
LENGTH = 43008


def shard_levels(key, shape, cuts, least, high):
    loudness = 1.0
    for dim, parts in cuts:
        heights = jax.random.uniform(jax.random.fold_in(jax.random.fold_in(key, 6), dim), (parts,), jnp.float32, least / len(cuts), high / len(cuts))
        loudness = loudness * jnp.repeat(jnp.exp(heights), shape[dim] // parts).reshape((-1,) + (1,) * (len(shape) - 1 - dim))
    return loudness


def gaussian(rng, shape, spread, bound, pieces=(), held_as=jnp.bfloat16):
    entries = jax.random.normal(rng, shape, jnp.float32) * spread
    if len(pieces) > 0:
        entries = shard_levels(rng, shape, pieces, -0.22, 0.18) * entries
    return jnp.clip(entries, min=-bound, max=bound).astype(held_as)


def setup_inputs(seed: int = 0) -> dict:
    keys = jax.random.split(jax.random.key(seed), 7)
    tokens = gaussian(keys[0], (LENGTH, C), 1.0, 6.0, ((0, 16), (1, 8)))
    conv_weight = gaussian(keys[1], (LAYERS, 3, C, C), (3 * C) ** -0.5, 0.109375, ((3, 8),))
    conv_bias = gaussian(keys[2], (LAYERS, C), 0.5, 3.0, ((1, 8),), jnp.float32)
    mix_weight = gaussian(keys[3], (LAYERS, C, C), C ** -0.5, 0.1875, ((2, 8),))
    mix_bias = gaussian(keys[4], (LAYERS, C), 0.5, 3.0, ((1, 8),), jnp.float32)
    norm_gain = jnp.clip(1.0 + 0.18 * jax.random.normal(keys[5], (LAYERS, C), jnp.float32), 0.1, 1.9)
    return {"tokens": tokens, "conv_weight": conv_weight, "conv_bias": conv_bias, "mix_weight": mix_weight, "mix_bias": mix_bias, "norm_gain": norm_gain}


def normalize(values, gain_row):
    widened = values.astype(jnp.float32)
    scale = lax.rsqrt(lax.optimization_barrier(jnp.mean(widened * widened, axis=-1, keepdims=True)) + 1e-06)
    return (widened * scale * gain_row).astype(jnp.bfloat16)

def reference(tokens, conv_weight, conv_bias, mix_weight, mix_bias, norm_gain):
    current = tokens
    for block_index in range(LAYERS):
        distance = POS_DEV * 2 ** block_index
        normed = normalize(current, norm_gain[block_index])
        padding = jnp.zeros((distance, C), jnp.bfloat16)
        earlier = jnp.concatenate([padding, normed[:-distance]], axis=0)
        following = jnp.concatenate([normed[distance:], padding], axis=0)
        hidden = jnp.dot(earlier, conv_weight[block_index, 0], preferred_element_type=jnp.float32)
        hidden = hidden + jnp.dot(normed, conv_weight[block_index, 1], preferred_element_type=jnp.float32)
        hidden = hidden + jnp.dot(following, conv_weight[block_index, 2], preferred_element_type=jnp.float32)
        hidden = hidden + conv_bias[block_index]
        activated = jax.nn.gelu(hidden, approximate=False).astype(jnp.bfloat16)
        mixed = jnp.dot(activated, mix_weight[block_index], preferred_element_type=jnp.float32) + mix_bias[block_index]
        current = (current.astype(jnp.float32) + mixed).astype(jnp.bfloat16)
    return current
```

```python
import functools

import jax
import jax.numpy as jnp
from jax import lax
from jax.experimental import pallas as pl
from jax.experimental.pallas import tpu as pltpu
from jax.sharding import PartitionSpec as P

LAYERS = 2
C = 1024
BLOCKS = 16
LANES = 128
SHARDS = 8
RES = 24
ROWS = BLOCKS * RES
EXTRA = 16
AXES = ("seq", "filt")


def coords(i):
    z, i = i % 4, i // 4
    yl, i = i % 2, i // 2
    c, i = i % 2, i // 2
    yh, x = i % 2, i // 2
    return x, yh * 2 + yl, z, c


def linear(x, y, z, c):
    x, y, z = x % 4, y % 4, z % 4
    return (((x * 2 + y // 2) * 2 + c) * 2 + y % 2) * 4 + z


def route(step):
    return [(i, linear(*step(*coords(i)))) for i in range(128)]


Z_AWAY = route(lambda x, y, z, c: (x, y, z + 1 - 2 * c, c))
Z_BACK = route(lambda x, y, z, c: (x, y, z - 1 + 2 * c, c))
Y_SIDE = route(lambda x, y, z, c: (x, y + 1 - 2 * c, z, c))
SWAP = route(lambda x, y, z, c: (x, y, z, 1 - c))


def send(block, path):
    return lax.ppermute(block, AXES, path)


def three_parts(v):
    hi = v.astype(jnp.bfloat16).astype(jnp.float32)
    mid = (v - hi).astype(jnp.bfloat16).astype(jnp.float32)
    lo = v - hi - mid
    return [hi, mid, lo]


def prepare_kernel(where_ref, tokens_ref, conv_ref, mix_ref, conv_bias_ref, mix_bias_ref, padded_ref, *rest):
    own, (zeros, bias, sems) = rest[:LAYERS], rest[LAYERS:]
    core = where_ref[0]
    length = tokens_ref.shape[0]
    moves = [(tokens_ref, padded_ref.at[pl.ds(0, length)])]
    for layer in range(LAYERS):
        moves.append((conv_ref.at[layer, 2 * core], own[layer].at[pl.ds(0, C)]))
    copies = [pltpu.make_async_copy(a, b, sems.at[i]) for i, (a, b) in enumerate(moves)]
    for copy in copies:
        copy.start()
    for layer in range(LAYERS):
        second = own[layer].at[pl.ds(C, C)]

        @pl.when(core == 0)
        def _(layer=layer, second=second):
            pltpu.make_async_copy(conv_ref.at[layer, 1], second, sems.at[5 + layer]).start()

        @pl.when(core == 1)
        def _(layer=layer, second=second):
            pltpu.make_async_copy(mix_ref.at[layer], second, sems.at[5 + layer]).start()

    zeros[...] = jnp.zeros_like(zeros)
    for layer in range(LAYERS):
        rows = three_parts(conv_bias_ref[layer:layer + 1, :]) + three_parts(mix_bias_ref[layer:layer + 1, :])
        rows.append(jnp.zeros((EXTRA - 6, LANES), jnp.float32))
        bias[layer] = jnp.concatenate(rows, axis=0).astype(jnp.bfloat16)
    late = [(zeros, padded_ref.at[pl.ds(length, 128 * RES - length)])]
    for layer in range(LAYERS):
        late.append((bias.at[layer], own[layer].at[pl.ds(2 * C, EXTRA)]))
    more = [pltpu.make_async_copy(a, b, sems.at[7 + i]) for i, (a, b) in enumerate(late)]
    for copy in more:
        copy.start()
    for copy in copies + more:
        copy.wait()
    for layer in range(LAYERS):
        pltpu.make_async_copy(mix_ref.at[layer], own[layer].at[pl.ds(C, C)], sems.at[5 + layer]).wait()


def prepare(where, tokens, conv, mix, conv_bias, mix_bias):
    anywhere = pl.BlockSpec(memory_space=pl.ANY)
    hbm = pl.BlockSpec(memory_space=pltpu.HBM)
    vmem = pl.BlockSpec(memory_space=pltpu.VMEM)
    half = jax.ShapeDtypeStruct((2 * C + EXTRA, LANES), jnp.bfloat16)
    return pl.pallas_call(
        prepare_kernel,
        out_shape=[jax.ShapeDtypeStruct((128 * RES, LANES), jnp.bfloat16)] + [half] * LAYERS,
        in_specs=[pl.BlockSpec(memory_space=pltpu.SMEM), hbm, hbm, hbm, vmem, vmem],
        out_specs=[anywhere] * (1 + LAYERS),
        scratch_shapes=[
            pltpu.VMEM((128 * RES - tokens.shape[0], LANES), jnp.bfloat16),
            pltpu.VMEM((LAYERS, EXTRA, LANES), jnp.bfloat16),
            pltpu.SemaphoreType.DMA((7 + 1 + LAYERS,)),
        ],
        compiler_params=pltpu.CompilerParams(vmem_limit_bytes=4 * 2**20),
        cost_estimate=pl.CostEstimate(flops=0, bytes_accessed=4 * 2**20, transcendentals=0),
        name="prepare",
    )(where, tokens, conv, mix, conv_bias, mix_bias)


def layer_kernel(layer, first, last, where_ref, x_ref, gain_ref, conv_ref, mix_ref, own_ref, *rest):
    mine, other = rest[:7], rest[7:14]
    out_ref = rest[14]
    w, bias, x, n, act, sems, bias_sems = rest[15:]
    core = where_ref[0]

    def strip(k):
        return pl.ds(k * LANES, LANES)

    def home(k):
        return pl.ds(pl.multiple_of(where_ref[1 + k] * LANES, LANES), LANES)

    for k in range(SHARDS):
        moves = []
        if k == 0:
            for t in range(3):
                moves.append((conv_ref.at[layer, t], t))
            moves.append((mix_ref.at[layer], 3))
            extra = own_ref
        else:
            for src, base in ((mine[k - 1], 2 * core), (other[k - 1], 2 - 2 * core)):
                for h in range(2):
                    moves.append((src.at[pl.ds(h * C, C)], base + h))
            extra = mine[k - 1]
        for src, t in moves:
            pltpu.make_async_copy(src, w.at[t, :, strip(k)], sems.at[t, k]).start()
        pltpu.make_async_copy(extra.at[pl.ds(2 * C, EXTRA)], bias.at[:, strip(k)], bias_sems.at[k]).start()

    def ready(t, k):
        pltpu.make_async_copy(mix_ref.at[layer], w.at[t, :, strip(k)], sems.at[t, k]).wait()

    if first:
        for b in range(BLOCKS):
            for f in range(SHARDS):
                x[b * RES:(b + 1) * RES, f * LANES:(f + 1) * LANES] = x_ref[b * SHARDS + f].astype(jnp.float32)
    else:
        x[...] = x_ref[...].astype(jnp.float32)
    wide = x[...]
    scale = lax.rsqrt(jnp.mean(wide * wide, axis=-1, keepdims=True) + 1e-06)
    n[...] = (wide * scale * gain_ref[layer:layer + 1, :]).astype(jnp.bfloat16)

    shift = RES * 2**layer
    width = 2 * LANES

    def bias_row(start, cols):
        parts = bias[:, cols].astype(jnp.float32)
        return parts[start:start + 1] + parts[start + 1:start + 2] + parts[start + 2:start + 3]

    for j in range(SHARDS // 2):
        cols = slice(j * width, (j + 1) * width)
        for k in (2 * j, 2 * j + 1):
            for t in range(3):
                ready(t, k)
            pltpu.make_async_copy(own_ref.at[pl.ds(2 * C, EXTRA)], bias.at[:, strip(k)], bias_sems.at[k]).wait()
        hidden = jnp.dot(n[...], w[1, :, cols], preferred_element_type=jnp.float32) + bias_row(0, cols)
        edge = jnp.zeros((shift, width), jnp.float32)
        earlier = jnp.dot(n[...], w[0, :, cols], preferred_element_type=jnp.float32)
        hidden = hidden + jnp.concatenate([edge, earlier[:ROWS - shift]], axis=0)
        later = jnp.dot(n[...], w[2, :, cols], preferred_element_type=jnp.float32)
        hidden = hidden + jnp.concatenate([later[shift:], edge], axis=0)
        done = (hidden * (1.0 + lax.erf(hidden * 0.7071067811865476)) * 0.5).astype(jnp.bfloat16)
        for h in range(2):
            act[:, home(2 * j + h)] = done[:, h * LANES:(h + 1) * LANES]

    for j in range(SHARDS // 2):
        cols = slice(j * width, (j + 1) * width)
        for k in (2 * j, 2 * j + 1):
            ready(3, k)
        mixed = jnp.dot(act[...], w[3, :, cols], preferred_element_type=jnp.float32) + bias_row(3, cols)
        for h in range(2):
            k = 2 * j + h
            total = (x[:, home(k)] + mixed[:, h * LANES:(h + 1) * LANES]).astype(jnp.bfloat16)
            if last:
                f = where_ref[1 + k]
                for b in range(BLOCKS):
                    out_ref[b * SHARDS + f] = total[b * RES:(b + 1) * RES]
            else:
                out_ref[:, home(k)] = total


def run_layer(layer, where, x, gain, conv, mix, own, mine, other):
    first, last = layer == 0, layer == LAYERS - 1
    anywhere = pl.BlockSpec(memory_space=pl.ANY)
    hbm = pl.BlockSpec(memory_space=pltpu.HBM)
    vmem = pl.BlockSpec(memory_space=pltpu.VMEM)
    out = (BLOCKS * SHARDS, RES, LANES) if last else (ROWS, C)
    return pl.pallas_call(
        functools.partial(layer_kernel, layer, first, last),
        out_shape=jax.ShapeDtypeStruct(out, jnp.bfloat16),
        in_specs=[pl.BlockSpec(memory_space=pltpu.SMEM), vmem, vmem, hbm, hbm] + [anywhere] * 15,
        out_specs=vmem,
        scratch_shapes=[
            pltpu.VMEM((4, C, C), jnp.bfloat16),
            pltpu.VMEM((EXTRA, C), jnp.bfloat16),
            pltpu.VMEM((ROWS, C), jnp.float32),
            pltpu.VMEM((ROWS, C), jnp.bfloat16),
            pltpu.VMEM((ROWS, C), jnp.bfloat16),
            pltpu.SemaphoreType.DMA((4, SHARDS)),
            pltpu.SemaphoreType.DMA((SHARDS,)),
        ],
        compiler_params=pltpu.CompilerParams(vmem_limit_bytes=20 * 2**20),
        cost_estimate=pl.CostEstimate(flops=8 * ROWS * C * C, bytes_accessed=9 * 2**20, transcendentals=ROWS * C),
        name=f"layer{layer}",
    )(where, x, gain, conv, mix, own, *mine, *other)


def per_device(tokens, conv_weight, conv_bias, mix_weight, mix_bias, norm_gain):
    seq, filt = lax.axis_index("seq"), lax.axis_index("filt")
    core = seq & 1
    z, yl = filt & 3, filt >> 2
    zs = [z, (z - 1 + 2 * core) & 3, (z + 1 - 2 * core) & 3, (z + 2) & 3]
    shards = [yl * 4 + v for v in zs] + [(1 - yl) * 4 + v for v in zs]
    where = jnp.stack([core] + shards).astype(jnp.int32)

    padded, *owns = prepare(where, tokens, conv_weight, mix_weight, conv_bias, mix_bias)
    x = lax.all_to_all(padded.reshape(128, RES, LANES), AXES, split_axis=0, concat_axis=0, tiled=True)

    gathered = []
    for layer in range(LAYERS):
        own = owns[layer]
        if layer > 0:
            own, x, near, far = lax.optimization_barrier((own, x, near, far))
            gathered[0][1][0], gathered[0][1][1] = near, far
        near = send(own, Z_AWAY)
        far = send(own, Z_BACK)
        beyond = send(near, Z_AWAY)
        same = [own, near, far, beyond]
        cross = [send(v, Y_SIDE) for v in same]
        mine = same[1:] + cross
        other_core = [send(v, SWAP) for v in mine]
        gathered.append((own, mine, other_core))

    for layer in range(LAYERS):
        own, mine, other = gathered[layer]
        order = [1, 0, 2, 3, 5, 4, 6]
        x = run_layer(layer, where, x, norm_gain, conv_weight, mix_weight, own, mine, [other[i] for i in order])
    y = lax.all_to_all(x, AXES, split_axis=0, concat_axis=0, tiled=True)
    return y.reshape(128 * RES, LANES)[:tokens.shape[0]]


def solution(mesh):
    in_specs = (
        P("seq", "filt"),
        P(None, None, None, "filt"),
        P(None, "filt"),
        P(None, None, "filt"),
        P(None, "filt"),
        P(),
    )
    out_specs = P("seq", "filt")
    return jax.shard_map(
        per_device, mesh=mesh, in_specs=in_specs, out_specs=out_specs, check_vma=False
    )
```

```python
import functools

import jax
import jax.numpy as jnp
from jax import lax
from jax.experimental import pallas as pl
from jax.experimental.pallas import tpu as pltpu
from jax.sharding import PartitionSpec as P

LAYERS = 2
C = 1024
BLOCKS = 16
LANES = 128
SHARDS = 8
RES = 24
ROWS = BLOCKS * RES
EXTRA = 16
QUARTER = C // 4
PART = C + EXTRA
AXES = ("seq", "filt")


def coords(i):
    z, i = i % 4, i // 4
    yl, i = i % 2, i // 2
    c, i = i % 2, i // 2
    yh, x = i % 2, i // 2
    return x, yh * 2 + yl, z, c


def linear(x, y, z, c):
    x, y, z = x % 4, y % 4, z % 4
    return (((x * 2 + y // 2) * 2 + c) * 2 + y % 2) * 4 + z


def route(step):
    return [(i, linear(*step(*coords(i)))) for i in range(128)]


Z_AWAY = route(lambda x, y, z, c: (x, y, z + 1 - 2 * c, c))
Z_BACK = route(lambda x, y, z, c: (x, y, z - 1 + 2 * c, c))
Y_SIDE = route(lambda x, y, z, c: (x, y + 1 - 2 * c, z, c))
X_SIDE = route(lambda x, y, z, c: (x + 1 - 2 * c, y, z, c))
SWAP = route(lambda x, y, z, c: (x, y, z, 1 - c))


def send(block, path):
    return lax.ppermute(block, AXES, path)


def three_parts(v):
    hi = v.astype(jnp.bfloat16).astype(jnp.float32)
    mid = (v - hi).astype(jnp.bfloat16).astype(jnp.float32)
    lo = v - hi - mid
    return [hi, mid, lo]


def prepare_kernel(where_ref, tokens_ref, conv_ref, mix_ref, conv_bias_ref, mix_bias_ref, padded_ref, first_ref, second_ref, zeros, bias, sems):
    length = tokens_ref.shape[0]
    moves = [(tokens_ref, padded_ref.at[pl.ds(0, length)])]
    for i, part in enumerate((first_ref, second_ref)):
        rows = pl.ds(pl.multiple_of(where_ref[i] * QUARTER, QUARTER), QUARTER)
        for layer in range(LAYERS):
            for t in range(4):
                source = conv_ref.at[layer, t, rows] if t < 3 else mix_ref.at[layer, rows]
                moves.append((source, part.at[pl.ds(layer * PART + t * QUARTER, QUARTER)]))
    copies = [pltpu.make_async_copy(a, b, sems.at[i]) for i, (a, b) in enumerate(moves)]
    for copy in copies:
        copy.start()
    zeros[...] = jnp.zeros_like(zeros)
    for layer in range(LAYERS):
        rows = three_parts(conv_bias_ref[layer:layer + 1, :]) + three_parts(mix_bias_ref[layer:layer + 1, :])
        rows.append(jnp.zeros((EXTRA - 6, LANES), jnp.float32))
        bias[layer] = jnp.concatenate(rows, axis=0).astype(jnp.bfloat16)
    late = [(zeros, padded_ref.at[pl.ds(length, 128 * RES - length)])]
    for part in (first_ref, second_ref):
        for layer in range(LAYERS):
            late.append((bias.at[layer], part.at[pl.ds(layer * PART + C, EXTRA)]))
    more = [pltpu.make_async_copy(a, b, sems.at[len(moves) + i]) for i, (a, b) in enumerate(late)]
    for copy in more:
        copy.start()
    for copy in copies + more:
        copy.wait()


def prepare(where, tokens, conv, mix, conv_bias, mix_bias):
    anywhere = pl.BlockSpec(memory_space=pl.ANY)
    vmem = pl.BlockSpec(memory_space=pltpu.VMEM)
    part = jax.ShapeDtypeStruct((LAYERS * PART, LANES), jnp.bfloat16)
    return pl.pallas_call(
        prepare_kernel,
        out_shape=[jax.ShapeDtypeStruct((128 * RES, LANES), jnp.bfloat16), part, part],
        in_specs=[pl.BlockSpec(memory_space=pltpu.SMEM), anywhere, anywhere, anywhere, vmem, vmem],
        out_specs=[anywhere] * 3,
        scratch_shapes=[
            pltpu.VMEM((128 * RES - tokens.shape[0], LANES), jnp.bfloat16),
            pltpu.VMEM((LAYERS, EXTRA, LANES), jnp.bfloat16),
            pltpu.SemaphoreType.DMA((2 + 12 * LAYERS,)),
        ],
        compiler_params=pltpu.CompilerParams(vmem_limit_bytes=60 * 2**20),
        cost_estimate=pl.CostEstimate(flops=0, bytes_accessed=4 * 2**20, transcendentals=0),
        name="prepare",
    )(where, tokens, conv, mix, conv_bias, mix_bias)


def blocks_kernel(where_ref, x_ref, gain_ref, conv_ref, mix_ref, own_ref, *rest):
    parts = rest[:4 * (SHARDS - 1)]
    out_ref, w, mine, bias, x, normed, n, act, mixing, sems, mine_sems, bias_sems = rest[4 * (SHARDS - 1):]
    width = 2 * LANES

    def quarter(i):
        return pl.ds(pl.multiple_of(where_ref[i] * QUARTER, QUARTER), QUARTER)

    def home(k):
        return pl.ds(pl.multiple_of(where_ref[4 + k] * LANES, LANES), LANES)

    arriving = []
    for layer in range(LAYERS):
        layer_rows = pl.ds(layer * PART, PART)
        for k in range(SHARDS):
            if k == 0:
                moves = [
                    (conv_ref.at[layer], mine.at[layer, pl.ds(0, 3)], mine_sems.at[layer, 0]),
                    (mix_ref.at[layer], mine.at[layer, 3], mine_sems.at[layer, 1]),
                    (own_ref.at[pl.ds(layer * PART + C, EXTRA)], bias.at[layer], bias_sems.at[layer]),
                ]
            else:
                moves = []
                for i in range(4):
                    p = 4 * (k - 1) + i
                    moves.append((parts[p].at[layer_rows], w.at[p, layer_rows], sems.at[layer, p]))
            copies = [pltpu.make_async_copy(*move) for move in moves]
            for copy in copies:
                copy.start()
            arriving.append(copies)

    for b in range(BLOCKS):
        for f in range(SHARDS):
            x[b * RES:(b + 1) * RES, f * LANES:(f + 1) * LANES] = x_ref[b * SHARDS + f].astype(jnp.float32)

    for layer in range(LAYERS):
        base = layer * PART
        wide = x[...]
        scale = lax.rsqrt(jnp.mean(wide * wide, axis=-1, keepdims=True) + 1e-06)
        normed[...] = wide * scale * gain_ref[layer:layer + 1, :]
        shift = RES * 2**layer
        edge = jnp.zeros((shift, QUARTER), jnp.float32)
        for i in range(4):
            here = normed[:, quarter(i)]
            earlier = jnp.concatenate([edge, here[:ROWS - shift]], axis=0)
            later = jnp.concatenate([here[shift:], edge], axis=0)
            for t, rows in enumerate((earlier, here, later)):
                start = (3 * i + t) * QUARTER
                n[:, start:start + QUARTER] = rows.astype(jnp.bfloat16)

        def conv_column(k):
            if k == 0:
                return jnp.concatenate([mine[layer, t, quarter(i), :] for i in range(4) for t in range(3)], axis=0)
            return jnp.concatenate([w[4 * (k - 1) + i, base:base + 3 * QUARTER, :] for i in range(4)], axis=0)

        def mix_column(k):
            if k == 0:
                return jnp.concatenate([mine[layer, 3, quarter(i), :] for i in range(4)], axis=0)
            return jnp.concatenate([w[4 * (k - 1) + i, base + 3 * QUARTER:base + C, :] for i in range(4)], axis=0)

        def bias_row(k, start):
            rows = bias[layer] if k == 0 else w[4 * (k - 1), base + C:base + PART, :]
            rows = rows.astype(jnp.float32)
            return rows[start:start + 1] + rows[start + 1:start + 2] + rows[start + 2:start + 3]

        for j in range(SHARDS // 2):
            pair = (2 * j, 2 * j + 1)
            for k in pair:
                for copy in arriving[layer * SHARDS + k]:
                    copy.wait()
            taps = jnp.concatenate([conv_column(k) for k in pair], axis=1)
            hidden = jnp.dot(n[...], taps, preferred_element_type=jnp.float32)
            hidden = hidden + jnp.concatenate([bias_row(k, 0) for k in pair], axis=1)
            done = (hidden * (1.0 + lax.erf(hidden * 0.7071067811865476)) * 0.5).astype(jnp.bfloat16)
            for h, k in enumerate(pair):
                act[:, home(k)] = done[:, h * LANES:(h + 1) * LANES]

        for i in range(4):
            mixing[:, i * QUARTER:(i + 1) * QUARTER] = act[:, quarter(i)]

        for j in range(SHARDS // 2):
            pair = (2 * j, 2 * j + 1)
            mixed = jnp.dot(mixing[...], jnp.concatenate([mix_column(k) for k in pair], axis=1), preferred_element_type=jnp.float32)
            mixed = mixed + jnp.concatenate([bias_row(k, 3) for k in pair], axis=1)
            for h, k in enumerate(pair):
                total = x[:, home(k)] + mixed[:, h * LANES:(h + 1) * LANES]
                if layer == LAYERS - 1:
                    f = where_ref[4 + k]
                    for b in range(BLOCKS):
                        out_ref[b * SHARDS + f] = total[b * RES:(b + 1) * RES].astype(jnp.bfloat16)
                else:
                    x[:, home(k)] = total.astype(jnp.bfloat16).astype(jnp.float32)


def run_blocks(where, x, gain, conv, mix, own, parts):
    vmem = pl.BlockSpec(memory_space=pltpu.VMEM)
    anywhere = pl.BlockSpec(memory_space=pl.ANY)
    return pl.pallas_call(
        blocks_kernel,
        out_shape=jax.ShapeDtypeStruct((BLOCKS * SHARDS, RES, LANES), jnp.bfloat16),
        in_specs=[pl.BlockSpec(memory_space=pltpu.SMEM), vmem, vmem] + [anywhere] * (3 + len(parts)),
        out_specs=vmem,
        scratch_shapes=[
            pltpu.VMEM((len(parts), LAYERS * PART, LANES), jnp.bfloat16),
            pltpu.VMEM((LAYERS, 4, C, LANES), jnp.bfloat16),
            pltpu.VMEM((LAYERS, EXTRA, LANES), jnp.bfloat16),
            pltpu.VMEM((ROWS, C), jnp.float32),
            pltpu.VMEM((ROWS, C), jnp.float32),
            pltpu.VMEM((ROWS, 3 * C), jnp.bfloat16),
            pltpu.VMEM((ROWS, C), jnp.bfloat16),
            pltpu.VMEM((ROWS, C), jnp.bfloat16),
            pltpu.SemaphoreType.DMA((LAYERS, len(parts))),
            pltpu.SemaphoreType.DMA((LAYERS, 2)),
            pltpu.SemaphoreType.DMA((LAYERS,)),
        ],
        compiler_params=pltpu.CompilerParams(vmem_limit_bytes=32 * 2**20),
        cost_estimate=pl.CostEstimate(flops=16 * ROWS * C * C, bytes_accessed=18 * 2**20, transcendentals=2 * ROWS * C),
        name="blocks",
    )(where, x, gain, conv, mix, own, *parts)


def per_device(tokens, conv_weight, conv_bias, mix_weight, mix_bias, norm_gain):
    seq, filt = lax.axis_index("seq"), lax.axis_index("filt")
    core, parity = seq & 1, (seq >> 2) & 1
    z, yl = filt & 3, filt >> 2
    quarters = [2 * core + parity, 2 * core + 1 - parity, 2 - 2 * core + parity, 3 - 2 * core - parity]
    zs = [z, (z - 1 + 2 * core) & 3, (z + 1 - 2 * core) & 3, (z + 2) & 3]
    shards = [yl * 4 + v for v in zs] + [(1 - yl) * 4 + v for v in zs]
    where = jnp.stack(quarters + shards).astype(jnp.int32)

    padded, own, own2 = prepare(where, tokens, conv_weight, mix_weight, conv_bias, mix_bias)
    near, far = send(own, Z_AWAY), send(own, Z_BACK)
    cross = send(own, Y_SIDE)
    x = lax.all_to_all(padded.reshape(128, RES, LANES), AXES, split_axis=0, concat_axis=0, tiled=True)
    own2, x = lax.optimization_barrier((own2, x))
    near2, far2 = send(own2, Z_AWAY), send(own2, Z_BACK)
    cross2 = send(own2, Y_SIDE)
    beyond = send(near, Z_AWAY)
    cross_near, cross_far = send(near, Y_SIDE), send(far, Y_SIDE)
    beyond2 = send(beyond, X_SIDE)
    cross_beyond = send(beyond, Y_SIDE)
    cross_near2, cross_far2, cross_beyond2 = [send(v, X_SIDE) for v in (cross_near, cross_far, cross_beyond)]
    mine = [
        (near, near2), (far, far2), (beyond, beyond2),
        (cross, cross2), (cross_near, cross_near2), (cross_far, cross_far2), (cross_beyond, cross_beyond2),
    ]
    swapped = [[send(v, SWAP) for v in pair] for pair in mine]
    parts = []
    for k, i in enumerate([1, 0, 2, 3, 5, 4, 6]):
        parts += list(mine[k]) + swapped[i]
    x = run_blocks(where, x, norm_gain, conv_weight, mix_weight, own, parts)
    y = lax.all_to_all(x, AXES, split_axis=0, concat_axis=0, tiled=True)
    return y.reshape(128 * RES, LANES)[:tokens.shape[0]]


def solution(mesh):
    in_specs = (
        P("seq", "filt"),
        P(None, None, None, "filt"),
        P(None, "filt"),
        P(None, None, "filt"),
        P(None, "filt"),
        P(),
    )
    out_specs = P("seq", "filt")
    return jax.shard_map(
        per_device, mesh=mesh, in_specs=in_specs, out_specs=out_specs, check_vma=False
    )
```

```python
import functools

import jax
import jax.numpy as jnp
from jax import lax
from jax.experimental import pallas as pl
from jax.experimental.pallas import tpu as pltpu
from jax.sharding import PartitionSpec as P

LAYERS = 2
C = 1024
BLOCKS = 16
LANES = 128
SHARDS = 8
RES = 24
ROWS = BLOCKS * RES
EXTRA = 16
HALF = C // 2
PART = 4 * HALF + EXTRA
AXES = ("seq", "filt")


def coords(i):
    z, i = i % 4, i // 4
    yl, i = i % 2, i // 2
    c, i = i % 2, i // 2
    yh, x = i % 2, i // 2
    return x, yh * 2 + yl, z, c


def linear(x, y, z, c):
    x, y, z = x % 4, y % 4, z % 4
    return (((x * 2 + y // 2) * 2 + c) * 2 + y % 2) * 4 + z


def route(step):
    return [(i, linear(*step(*coords(i)))) for i in range(128)]


Z_AWAY = route(lambda x, y, z, c: (x, y, z + 1 - 2 * c, c))
Z_BACK = route(lambda x, y, z, c: (x, y, z - 1 + 2 * c, c))
Y_SIDE = route(lambda x, y, z, c: (x, y + 1 - 2 * c, z, c))
SWAP = route(lambda x, y, z, c: (x, y, z, 1 - c))


def send(block, path):
    return lax.ppermute(block, AXES, path)


def three_parts(v):
    hi = v.astype(jnp.bfloat16).astype(jnp.float32)
    mid = (v - hi).astype(jnp.bfloat16).astype(jnp.float32)
    lo = v - hi - mid
    return [hi, mid, lo]


def prepare_kernel(where_ref, tokens_ref, conv_ref, mix_ref, conv_bias_ref, mix_bias_ref, padded_ref, own_ref, sems):
    length = tokens_ref.shape[0]
    rows = pl.ds(pl.multiple_of(where_ref[0] * HALF, HALF), HALF)
    moves = []
    for layer in range(LAYERS):
        for t in range(4):
            source = conv_ref.at[layer, t, rows] if t < 3 else mix_ref.at[layer, rows]
            moves.append((source, own_ref.at[pl.ds(layer * PART + t * HALF, HALF)]))
    moves.append((tokens_ref, padded_ref.at[pl.ds(0, length)]))
    copies = [pltpu.make_async_copy(a, b, sems.at[i]) for i, (a, b) in enumerate(moves)]
    for copy in copies:
        copy.start()
    padded_ref[length:, :] = jnp.zeros((128 * RES - length, LANES), jnp.bfloat16)
    for layer in range(LAYERS):
        lines = three_parts(conv_bias_ref[layer:layer + 1, :]) + three_parts(mix_bias_ref[layer:layer + 1, :])
        lines.append(jnp.zeros((EXTRA - 6, LANES), jnp.float32))
        own_ref[layer * PART + 4 * HALF:(layer + 1) * PART, :] = jnp.concatenate(lines, axis=0).astype(jnp.bfloat16)
    for copy in copies:
        copy.wait()


def prepare(where, tokens, conv, mix, conv_bias, mix_bias):
    anywhere = pl.BlockSpec(memory_space=pl.ANY)
    vmem = pl.BlockSpec(memory_space=pltpu.VMEM)
    return pl.pallas_call(
        prepare_kernel,
        out_shape=[
            jax.ShapeDtypeStruct((128 * RES, LANES), jnp.bfloat16),
            jax.ShapeDtypeStruct((LAYERS * PART, LANES), jnp.bfloat16),
        ],
        in_specs=[pl.BlockSpec(memory_space=pltpu.SMEM), anywhere, anywhere, anywhere, vmem, vmem],
        out_specs=[vmem, vmem],
        scratch_shapes=[pltpu.SemaphoreType.DMA((1 + 4 * LAYERS,))],
        compiler_params=pltpu.CompilerParams(vmem_limit_bytes=60 * 2**20),
        cost_estimate=pl.CostEstimate(flops=0, bytes_accessed=4 * 2**20, transcendentals=0),
        name="prepare",
    )(where, tokens, conv, mix, conv_bias, mix_bias)


def blocks_kernel(where_ref, x_ref, gain_ref, conv_ref, mix_ref, own_ref, *rest):
    parts = rest[:2 * (SHARDS - 1)]
    out_ref, w, mine, bias, x, normed, n, act, mixing, sems, mine_sems, bias_sems = rest[2 * (SHARDS - 1):]
    width = 2 * LANES

    def half(i):
        return pl.ds(pl.multiple_of(where_ref[i] * HALF, HALF), HALF)

    def home(k):
        return pl.ds(pl.multiple_of(where_ref[2 + k] * LANES, LANES), LANES)

    arriving = []
    for layer in range(LAYERS):
        layer_rows = pl.ds(layer * PART, PART)
        for k in range(SHARDS):
            if k == 0:
                moves = [
                    (conv_ref.at[layer], mine.at[layer, pl.ds(0, 3)], mine_sems.at[layer, 0]),
                    (mix_ref.at[layer], mine.at[layer, 3], mine_sems.at[layer, 1]),
                    (own_ref.at[pl.ds(layer * PART + 4 * HALF, EXTRA)], bias.at[layer], bias_sems.at[layer]),
                ]
            else:
                moves = []
                for i in range(2):
                    p = 2 * (k - 1) + i
                    moves.append((parts[p].at[layer_rows], w.at[p, layer_rows], sems.at[layer, p]))
            copies = [pltpu.make_async_copy(*move) for move in moves]
            for copy in copies:
                copy.start()
            arriving.append(copies)

    for b in range(BLOCKS):
        for f in range(SHARDS):
            x[b * RES:(b + 1) * RES, f * LANES:(f + 1) * LANES] = x_ref[b * SHARDS + f].astype(jnp.float32)

    for layer in range(LAYERS):
        base = layer * PART
        wide = x[...]
        scale = lax.rsqrt(jnp.mean(wide * wide, axis=-1, keepdims=True) + 1e-06)
        normed[...] = wide * scale * gain_ref[layer:layer + 1, :]
        shift = RES * 2**layer
        edge = jnp.zeros((shift, HALF), jnp.float32)
        for i in range(2):
            here = normed[:, half(i)]
            earlier = jnp.concatenate([edge, here[:ROWS - shift]], axis=0)
            later = jnp.concatenate([here[shift:], edge], axis=0)
            for t, rows in enumerate((earlier, here, later)):
                start = (3 * i + t) * HALF
                n[:, start:start + HALF] = rows.astype(jnp.bfloat16)

        def conv_column(k):
            if k == 0:
                return jnp.concatenate([mine[layer, t, half(i), :] for i in range(2) for t in range(3)], axis=0)
            return jnp.concatenate([w[2 * (k - 1) + i, base:base + 3 * HALF, :] for i in range(2)], axis=0)

        def mix_column(k):
            if k == 0:
                return jnp.concatenate([mine[layer, 3, half(i), :] for i in range(2)], axis=0)
            return jnp.concatenate([w[2 * (k - 1) + i, base + 3 * HALF:base + 4 * HALF, :] for i in range(2)], axis=0)

        def bias_row(k, start):
            rows = bias[layer] if k == 0 else w[2 * (k - 1), base + 4 * HALF:base + PART, :]
            rows = rows.astype(jnp.float32)
            return rows[start:start + 1] + rows[start + 1:start + 2] + rows[start + 2:start + 3]

        for j in range(SHARDS // 2):
            pair = (2 * j, 2 * j + 1)
            for k in pair:
                for copy in arriving[layer * SHARDS + k]:
                    copy.wait()
            taps = jnp.concatenate([conv_column(k) for k in pair], axis=1)
            hidden = jnp.dot(n[...], taps, preferred_element_type=jnp.float32)
            hidden = hidden + jnp.concatenate([bias_row(k, 0) for k in pair], axis=1)
            done = (hidden * (1.0 + lax.erf(hidden * 0.7071067811865476)) * 0.5).astype(jnp.bfloat16)
            for h, k in enumerate(pair):
                act[:, home(k)] = done[:, h * LANES:(h + 1) * LANES]

        for i in range(2):
            mixing[:, i * HALF:(i + 1) * HALF] = act[:, half(i)]

        for j in range(SHARDS // 2):
            pair = (2 * j, 2 * j + 1)
            mixed = jnp.dot(mixing[...], jnp.concatenate([mix_column(k) for k in pair], axis=1), preferred_element_type=jnp.float32)
            mixed = mixed + jnp.concatenate([bias_row(k, 3) for k in pair], axis=1)
            for h, k in enumerate(pair):
                total = x[:, home(k)] + mixed[:, h * LANES:(h + 1) * LANES]
                if layer == LAYERS - 1:
                    f = where_ref[2 + k]
                    for b in range(BLOCKS):
                        out_ref[b * SHARDS + f] = total[b * RES:(b + 1) * RES].astype(jnp.bfloat16)
                else:
                    x[:, home(k)] = total.astype(jnp.bfloat16).astype(jnp.float32)


def run_blocks(where, x, gain, conv, mix, own, parts):
    vmem = pl.BlockSpec(memory_space=pltpu.VMEM)
    anywhere = pl.BlockSpec(memory_space=pl.ANY)
    return pl.pallas_call(
        blocks_kernel,
        out_shape=jax.ShapeDtypeStruct((BLOCKS * SHARDS, RES, LANES), jnp.bfloat16),
        in_specs=[pl.BlockSpec(memory_space=pltpu.SMEM), vmem, vmem] + [anywhere] * (3 + len(parts)),
        out_specs=vmem,
        scratch_shapes=[
            pltpu.VMEM((len(parts), LAYERS * PART, LANES), jnp.bfloat16),
            pltpu.VMEM((LAYERS, 4, C, LANES), jnp.bfloat16),
            pltpu.VMEM((LAYERS, EXTRA, LANES), jnp.bfloat16),
            pltpu.VMEM((ROWS, C), jnp.float32),
            pltpu.VMEM((ROWS, C), jnp.float32),
            pltpu.VMEM((ROWS, 3 * C), jnp.bfloat16),
            pltpu.VMEM((ROWS, C), jnp.bfloat16),
            pltpu.VMEM((ROWS, C), jnp.bfloat16),
            pltpu.SemaphoreType.DMA((LAYERS, len(parts))),
            pltpu.SemaphoreType.DMA((LAYERS, 2)),
            pltpu.SemaphoreType.DMA((LAYERS,)),
        ],
        compiler_params=pltpu.CompilerParams(vmem_limit_bytes=32 * 2**20),
        cost_estimate=pl.CostEstimate(flops=16 * ROWS * C * C, bytes_accessed=18 * 2**20, transcendentals=2 * ROWS * C),
        name="blocks",
    )(where, x, gain, conv, mix, own, *parts)


def per_device(tokens, conv_weight, conv_bias, mix_weight, mix_bias, norm_gain):
    seq, filt = lax.axis_index("seq"), lax.axis_index("filt")
    core = seq & 1
    z, yl = filt & 3, filt >> 2
    zs = [z, (z - 1 + 2 * core) & 3, (z + 1 - 2 * core) & 3, (z + 2) & 3]
    shards = [yl * 4 + v for v in zs] + [(1 - yl) * 4 + v for v in zs]
    where = jnp.stack([core, 1 - core] + shards).astype(jnp.int32)

    padded, own = prepare(where, tokens, conv_weight, mix_weight, conv_bias, mix_bias)
    near, far = send(own, Z_AWAY), send(own, Z_BACK)
    cross = send(own, Y_SIDE)
    x = lax.all_to_all(padded.reshape(128, RES, LANES), AXES, split_axis=0, concat_axis=0, tiled=True)
    near, far, cross, x = lax.optimization_barrier((near, far, cross, x))
    beyond = send(near, Z_AWAY)
    cross_near = send(near, Y_SIDE)
    far, cross_near = lax.optimization_barrier((far, cross_near))
    cross_far = send(far, Y_SIDE)
    cross_beyond = send(cross_near, Z_AWAY)
    mine = [near, far, beyond, cross, cross_near, cross_far, cross_beyond]
    swapped = [send(v, SWAP) for v in mine]
    parts = []
    for k, i in enumerate([1, 0, 2, 3, 5, 4, 6]):
        parts += [mine[k], swapped[i]]
    x = run_blocks(where, x, norm_gain, conv_weight, mix_weight, own, parts)
    y = lax.all_to_all(x, AXES, split_axis=0, concat_axis=0, tiled=True)
    return y.reshape(128 * RES, LANES)[:tokens.shape[0]]


def solution(mesh):
    in_specs = (
        P("seq", "filt"),
        P(None, None, None, "filt"),
        P(None, "filt"),
        P(None, None, "filt"),
        P(None, "filt"),
        P(),
    )
    out_specs = P("seq", "filt")
    return jax.shard_map(
        per_device, mesh=mesh, in_specs=in_specs, out_specs=out_specs, check_vma=False
    )
```

```python
import functools

import jax
import jax.numpy as jnp
from jax import lax
from jax.experimental import pallas as pl
from jax.experimental.pallas import tpu as pltpu
from jax.sharding import PartitionSpec as P

LAYERS = 2
C = 1024
BLOCKS = 16
LANES = 128
SHARDS = 8
RES = 24
ROWS = BLOCKS * RES
EXTRA = 16
HALF = C // 2
PART = 4 * HALF + EXTRA
AXES = ("seq", "filt")


def coords(i):
    z, i = i % 4, i // 4
    yl, i = i % 2, i // 2
    c, i = i % 2, i // 2
    yh, x = i % 2, i // 2
    return x, yh * 2 + yl, z, c


def linear(x, y, z, c):
    x, y, z = x % 4, y % 4, z % 4
    return (((x * 2 + y // 2) * 2 + c) * 2 + y % 2) * 4 + z


def route(step):
    return [(i, linear(*step(*coords(i)))) for i in range(128)]


Z_AWAY = route(lambda x, y, z, c: (x, y, z + 1 - 2 * c, c))
Z_BACK = route(lambda x, y, z, c: (x, y, z - 1 + 2 * c, c))
Y_SIDE = route(lambda x, y, z, c: (x, y + 1 - 2 * c, z, c))
SWAP = route(lambda x, y, z, c: (x, y, z, 1 - c))


def send(block, path):
    return lax.ppermute(block, AXES, path)


def three_parts(v):
    hi = v.astype(jnp.bfloat16).astype(jnp.float32)
    mid = (v - hi).astype(jnp.bfloat16).astype(jnp.float32)
    lo = v - hi - mid
    return [hi, mid, lo]


def prepare_kernel(where_ref, tokens_ref, conv_ref, mix_ref, conv_bias_ref, mix_bias_ref, padded_ref, own_ref, *rest):
    singles, sems = rest[:LAYERS], rest[LAYERS]
    length = tokens_ref.shape[0]
    rows = pl.ds(pl.multiple_of(where_ref[0] * HALF, HALF), HALF)
    moves = []
    for layer in range(LAYERS):
        for t in range(4):
            source = conv_ref.at[layer, t, rows] if t < 3 else mix_ref.at[layer, rows]
            moves.append((source, own_ref.at[pl.ds(layer * PART + t * HALF, HALF)]))
            moves.append((source, singles[layer].at[pl.ds(t * HALF, HALF)]))
    moves.append((tokens_ref, padded_ref.at[pl.ds(0, length)]))
    copies = [pltpu.make_async_copy(a, b, sems.at[i]) for i, (a, b) in enumerate(moves)]
    for copy in copies:
        copy.start()
    padded_ref[length:, :] = jnp.zeros((128 * RES - length, LANES), jnp.bfloat16)
    for layer in range(LAYERS):
        lines = three_parts(conv_bias_ref[layer:layer + 1, :]) + three_parts(mix_bias_ref[layer:layer + 1, :])
        lines.append(jnp.zeros((EXTRA - 6, LANES), jnp.float32))
        block = jnp.concatenate(lines, axis=0).astype(jnp.bfloat16)
        own_ref[layer * PART + 4 * HALF:(layer + 1) * PART, :] = block
        singles[layer][4 * HALF:, :] = block
    for copy in copies:
        copy.wait()


def prepare(where, tokens, conv, mix, conv_bias, mix_bias):
    anywhere = pl.BlockSpec(memory_space=pl.ANY)
    vmem = pl.BlockSpec(memory_space=pltpu.VMEM)
    single = jax.ShapeDtypeStruct((PART, LANES), jnp.bfloat16)
    return pl.pallas_call(
        prepare_kernel,
        out_shape=[
            jax.ShapeDtypeStruct((128 * RES, LANES), jnp.bfloat16),
            jax.ShapeDtypeStruct((LAYERS * PART, LANES), jnp.bfloat16),
        ] + [single] * LAYERS,
        in_specs=[pl.BlockSpec(memory_space=pltpu.SMEM), anywhere, anywhere, anywhere, vmem, vmem],
        out_specs=[vmem] * (2 + LAYERS),
        scratch_shapes=[pltpu.SemaphoreType.DMA((1 + 8 * LAYERS,))],
        compiler_params=pltpu.CompilerParams(vmem_limit_bytes=60 * 2**20),
        cost_estimate=pl.CostEstimate(flops=0, bytes_accessed=6 * 2**20, transcendentals=0),
        name="prepare",
    )(where, tokens, conv, mix, conv_bias, mix_bias)


def layer_kernel(layer, bases, where_ref, x_ref, gain_ref, conv_ref, mix_ref, *rest):
    parts = rest[:2 * SHARDS - 1]
    out_ref, w, mine, bias, x, normed, n, act, mixing, sems, mine_sems, bias_sem = rest[2 * SHARDS - 1:]
    width = 2 * LANES
    first, last = layer == 0, layer == LAYERS - 1

    def half(i):
        return pl.ds(pl.multiple_of(where_ref[i] * HALF, HALF), HALF)

    def home(k):
        return pl.ds(pl.multiple_of(where_ref[2 + k] * LANES, LANES), LANES)

    arriving = []
    for k in range(SHARDS):
        if k == 0:
            moves = [
                (conv_ref.at[layer], mine.at[pl.ds(0, 3)], mine_sems.at[0]),
                (mix_ref.at[layer], mine.at[3], mine_sems.at[1]),
                (parts[0].at[pl.ds(bases[0] + 4 * HALF, EXTRA)], bias, bias_sem.at[0]),
            ]
        else:
            moves = []
            for p in (2 * k - 1, 2 * k):
                moves.append((parts[p].at[pl.ds(bases[p], PART)], w.at[p - 1], sems.at[p - 1]))
        copies = [pltpu.make_async_copy(*move) for move in moves]
        for copy in copies:
            copy.start()
        arriving.append(copies)

    if first:
        for b in range(BLOCKS):
            for f in range(SHARDS):
                x[b * RES:(b + 1) * RES, f * LANES:(f + 1) * LANES] = x_ref[b * SHARDS + f].astype(jnp.float32)
    else:
        x[...] = x_ref[...].astype(jnp.float32)
    wide = x[...]
    scale = lax.rsqrt(jnp.mean(wide * wide, axis=-1, keepdims=True) + 1e-06)
    normed[...] = wide * scale * gain_ref[layer:layer + 1, :]
    shift = RES * 2**layer
    edge = jnp.zeros((shift, HALF), jnp.float32)
    for i in range(2):
        here = normed[:, half(i)]
        earlier = jnp.concatenate([edge, here[:ROWS - shift]], axis=0)
        later = jnp.concatenate([here[shift:], edge], axis=0)
        for t, rows in enumerate((earlier, here, later)):
            start = (3 * i + t) * HALF
            n[:, start:start + HALF] = rows.astype(jnp.bfloat16)

    def conv_column(k):
        if k == 0:
            return jnp.concatenate([mine[t, half(i), :] for i in range(2) for t in range(3)], axis=0)
        return jnp.concatenate([w[2 * (k - 1) + i, :3 * HALF, :] for i in range(2)], axis=0)

    def mix_column(k):
        if k == 0:
            return jnp.concatenate([mine[3, half(i), :] for i in range(2)], axis=0)
        return jnp.concatenate([w[2 * (k - 1) + i, 3 * HALF:4 * HALF, :] for i in range(2)], axis=0)

    def bias_row(k, start):
        rows = bias[...] if k == 0 else w[2 * (k - 1), 4 * HALF:PART, :]
        rows = rows.astype(jnp.float32)
        return rows[start:start + 1] + rows[start + 1:start + 2] + rows[start + 2:start + 3]

    for j in range(SHARDS // 2):
        pair = (2 * j, 2 * j + 1)
        for k in pair:
            for copy in arriving[k]:
                copy.wait()
        taps = jnp.concatenate([conv_column(k) for k in pair], axis=1)
        hidden = jnp.dot(n[...], taps, preferred_element_type=jnp.float32)
        hidden = hidden + jnp.concatenate([bias_row(k, 0) for k in pair], axis=1)
        done = (hidden * (1.0 + lax.erf(hidden * 0.7071067811865476)) * 0.5).astype(jnp.bfloat16)
        for h, k in enumerate(pair):
            act[:, home(k)] = done[:, h * LANES:(h + 1) * LANES]

    for i in range(2):
        mixing[:, i * HALF:(i + 1) * HALF] = act[:, half(i)]

    for j in range(SHARDS // 2):
        pair = (2 * j, 2 * j + 1)
        mixed = jnp.dot(mixing[...], jnp.concatenate([mix_column(k) for k in pair], axis=1), preferred_element_type=jnp.float32)
        mixed = mixed + jnp.concatenate([bias_row(k, 3) for k in pair], axis=1)
        for h, k in enumerate(pair):
            total = x[:, home(k)] + mixed[:, h * LANES:(h + 1) * LANES]
            if last:
                f = where_ref[2 + k]
                for b in range(BLOCKS):
                    out_ref[b * SHARDS + f] = total[b * RES:(b + 1) * RES].astype(jnp.bfloat16)
            else:
                out_ref[:, home(k)] = total.astype(jnp.bfloat16)


def run_layer(layer, where, x, gain, conv, mix, parts, bases):
    vmem = pl.BlockSpec(memory_space=pltpu.VMEM)
    anywhere = pl.BlockSpec(memory_space=pl.ANY)
    out = (BLOCKS * SHARDS, RES, LANES) if layer == LAYERS - 1 else (ROWS, C)
    return pl.pallas_call(
        functools.partial(layer_kernel, layer, bases),
        out_shape=jax.ShapeDtypeStruct(out, jnp.bfloat16),
        in_specs=[pl.BlockSpec(memory_space=pltpu.SMEM), vmem, vmem] + [anywhere] * (2 + len(parts)),
        out_specs=vmem,
        scratch_shapes=[
            pltpu.VMEM((len(parts) - 1, PART, LANES), jnp.bfloat16),
            pltpu.VMEM((4, C, LANES), jnp.bfloat16),
            pltpu.VMEM((EXTRA, LANES), jnp.bfloat16),
            pltpu.VMEM((ROWS, C), jnp.float32),
            pltpu.VMEM((ROWS, C), jnp.float32),
            pltpu.VMEM((ROWS, 3 * C), jnp.bfloat16),
            pltpu.VMEM((ROWS, C), jnp.bfloat16),
            pltpu.VMEM((ROWS, C), jnp.bfloat16),
            pltpu.SemaphoreType.DMA((len(parts) - 1,)),
            pltpu.SemaphoreType.DMA((2,)),
            pltpu.SemaphoreType.DMA((1,)),
        ],
        compiler_params=pltpu.CompilerParams(vmem_limit_bytes=24 * 2**20),
        cost_estimate=pl.CostEstimate(flops=8 * ROWS * C * C, bytes_accessed=9 * 2**20, transcendentals=ROWS * C),
        name=f"layer{layer}",
    )(where, x, gain, conv, mix, *parts)


def per_device(tokens, conv_weight, conv_bias, mix_weight, mix_bias, norm_gain):
    seq, filt = lax.axis_index("seq"), lax.axis_index("filt")
    core = seq & 1
    z, yl = filt & 3, filt >> 2
    zs = [z, (z - 1 + 2 * core) & 3, (z + 1 - 2 * core) & 3, (z + 2) & 3]
    shards = [yl * 4 + v for v in zs] + [(1 - yl) * 4 + v for v in zs]
    where = jnp.stack([core, 1 - core] + shards).astype(jnp.int32)

    padded, own, *single = prepare(where, tokens, conv_weight, mix_weight, conv_bias, mix_bias)
    near = [send(v, Z_AWAY) for v in single]
    far = [send(v, Z_BACK) for v in single]
    cross = send(own, Y_SIDE)
    x = lax.all_to_all(padded.reshape(128, RES, LANES), AXES, split_axis=0, concat_axis=0, tiled=True)
    near, far, cross, x = lax.optimization_barrier((near, far, cross, x))
    swapped_cross = send(cross, SWAP)
    for layer in range(LAYERS):
        beyond = send(near[layer], Z_AWAY)
        cross_near = send(near[layer], Y_SIDE)
        far[layer], cross_near, beyond, x = lax.optimization_barrier((far[layer], cross_near, beyond, x))
        cross_far = send(far[layer], Y_SIDE)
        cross_beyond = send(cross_near, Z_AWAY)
        if layer + 1 < LAYERS:
            cross_far, cross_beyond, near[layer + 1] = lax.optimization_barrier((cross_far, cross_beyond, near[layer + 1]))
        mine = [near[layer], far[layer], beyond, cross, cross_near, cross_far, cross_beyond]
        swapped = [swapped_cross if v is cross else send(v, SWAP) for v in mine]
        parts, bases = [single[layer]], [0]
        for k, i in enumerate([1, 0, 2, 3, 5, 4, 6]):
            parts += [mine[k], swapped[i]]
            bases += [layer * PART if mine[k] is cross else 0] * 2
        x = run_layer(layer, where, x, norm_gain, conv_weight, mix_weight, parts, bases)
    y = lax.all_to_all(x, AXES, split_axis=0, concat_axis=0, tiled=True)
    return y.reshape(128 * RES, LANES)[:tokens.shape[0]]


def solution(mesh):
    in_specs = (
        P("seq", "filt"),
        P(None, None, None, "filt"),
        P(None, "filt"),
        P(None, None, "filt"),
        P(None, "filt"),
        P(),
    )
    out_specs = P("seq", "filt")
    return jax.shard_map(
        per_device, mesh=mesh, in_specs=in_specs, out_specs=out_specs, check_vma=False
    )
```

```python
import functools

import jax
import jax.numpy as jnp
from jax import lax
from jax.experimental import pallas as pl
from jax.experimental.pallas import tpu as pltpu
from jax.sharding import PartitionSpec as P

LAYERS = 2
C = 1024
BLOCKS = 16
LANES = 128
SHARDS = 8
RES = 24
ROWS = BLOCKS * RES
EXTRA = 16
HALF = C // 2
PART = 4 * HALF + EXTRA
AXES = ("seq", "filt")


def coords(i):
    z, i = i % 4, i // 4
    yl, i = i % 2, i // 2
    c, i = i % 2, i // 2
    yh, x = i % 2, i // 2
    return x, yh * 2 + yl, z, c


def linear(x, y, z, c):
    x, y, z = x % 4, y % 4, z % 4
    return (((x * 2 + y // 2) * 2 + c) * 2 + y % 2) * 4 + z


def route(step):
    return [(i, linear(*step(*coords(i)))) for i in range(128)]


Z_SIDE = route(lambda x, y, z, c: (x, y, z + 1 - 2 * (c ^ x & 1), c))
Y_SIDE = route(lambda x, y, z, c: (x, y + 1 - 2 * c, z, c))
X_SIDE = route(lambda x, y, z, c: (x + 1 - 2 * c, y, z, c))
SWAP = route(lambda x, y, z, c: (x, y, z, 1 - c))


def place():
    seq, filt = lax.axis_index("seq"), lax.axis_index("filt")
    core, parity = seq & 1, (seq >> 2) & 1
    z, yl = filt & 3, filt >> 2
    side = 2 * (core ^ parity) - 1
    zs = [z, (z + side) & 3, (z - side) & 3, (z + 2) & 3]
    return core, [yl * 4 + v for v in zs] + [(1 - yl) * 4 + v for v in zs]


def send(block, path):
    return lax.ppermute(block, AXES, path)


def three_parts(v):
    hi = v.astype(jnp.bfloat16).astype(jnp.float32)
    mid = (v - hi).astype(jnp.bfloat16).astype(jnp.float32)
    lo = v - hi - mid
    return [hi, mid, lo]


def prepare_kernel(tokens_ref, conv_ref, mix_ref, conv_bias_ref, mix_bias_ref, padded_ref, own_ref, bias_ref, tokens, own, sems, out_sems):
    length = tokens_ref.shape[0]
    core, _ = place()
    rows = pl.ds(pl.multiple_of(core * HALF, HALF), HALF)
    arriving, leaving = [], []
    for layer in range(LAYERS):
        for t in range(4):
            source = conv_ref.at[layer, t, rows] if t < 3 else mix_ref.at[layer, rows]
            spot = pl.ds(layer * PART + t * HALF, HALF)
            arriving.append((source, own.at[spot]))
            leaving.append((own.at[spot], own_ref.at[spot]))
    arriving.append((tokens_ref, tokens.at[pl.ds(0, length)]))
    leaving.append((tokens, padded_ref))
    arriving = [pltpu.make_async_copy(a, b, sems.at[i]) for i, (a, b) in enumerate(arriving)]
    for copy in arriving:
        copy.start()
    tokens[length:, :] = jnp.zeros((128 * RES - length, LANES), jnp.bfloat16)
    for layer in range(LAYERS):
        lines = three_parts(conv_bias_ref[layer:layer + 1, :]) + three_parts(mix_bias_ref[layer:layer + 1, :])
        lines.append(jnp.zeros((EXTRA - 6, LANES), jnp.float32))
        block = jnp.concatenate(lines, axis=0).astype(jnp.bfloat16)
        spot = slice(layer * PART + 4 * HALF, (layer + 1) * PART)
        own[spot, :] = block
        bias_ref[layer] = block
        leaving.append((own.at[spot], own_ref.at[spot]))
    leaving = [pltpu.make_async_copy(a, b, out_sems.at[i]) for i, (a, b) in enumerate(leaving)]
    for copy in leaving[len(arriving):]:
        copy.start()
    for coming, going in zip(arriving, leaving):
        coming.wait()
        going.start()
    for copy in leaving:
        copy.wait()


def prepare(tokens, conv, mix, conv_bias, mix_bias):
    anywhere = pl.BlockSpec(memory_space=pl.ANY)
    vmem = pl.BlockSpec(memory_space=pltpu.VMEM)
    return pl.pallas_call(
        prepare_kernel,
        out_shape=[
            jax.ShapeDtypeStruct((128 * RES, LANES), jnp.bfloat16),
            jax.ShapeDtypeStruct((LAYERS * PART, LANES), jnp.bfloat16),
            jax.ShapeDtypeStruct((LAYERS, EXTRA, LANES), jnp.bfloat16),
        ],
        in_specs=[anywhere, anywhere, anywhere, vmem, vmem],
        out_specs=[anywhere, anywhere, vmem],
        scratch_shapes=[
            pltpu.VMEM((128 * RES, LANES), jnp.bfloat16),
            pltpu.VMEM((LAYERS * PART, LANES), jnp.bfloat16),
            pltpu.SemaphoreType.DMA((1 + 4 * LAYERS,)),
            pltpu.SemaphoreType.DMA((1 + 5 * LAYERS,)),
        ],
        compiler_params=pltpu.CompilerParams(vmem_limit_bytes=60 * 2**20),
        cost_estimate=pl.CostEstimate(flops=0, bytes_accessed=4 * 2**20, transcendentals=0),
        name="prepare",
    )(tokens, conv, mix, conv_bias, mix_bias)


def blocks_kernel(x_ref, gain_ref, bias_ref, conv_ref, mix_ref, *rest):
    parts = rest[:2 * (SHARDS - 1)]
    out_ref, w, mine, x, normed, n, act, mixing, sems, mine_sems = rest[2 * (SHARDS - 1):]
    core, homes = place()
    halves = (core, 1 - core)
    width = 2 * LANES

    def half(i):
        return pl.ds(pl.multiple_of(halves[i] * HALF, HALF), HALF)

    def home(k):
        return pl.ds(pl.multiple_of(homes[k] * LANES, LANES), LANES)

    arriving = []
    for layer in range(LAYERS):
        layer_rows = pl.ds(layer * PART, PART)
        for k in range(SHARDS):
            if k == 0:
                moves = [
                    (conv_ref.at[layer], mine.at[layer, pl.ds(0, 3)], mine_sems.at[layer, 0]),
                    (mix_ref.at[layer], mine.at[layer, 3], mine_sems.at[layer, 1]),
                ]
            else:
                moves = []
                for i in range(2):
                    p = 2 * (k - 1) + i
                    moves.append((parts[p].at[layer_rows], w.at[p, layer_rows], sems.at[layer, p]))
            copies = [pltpu.make_async_copy(*move) for move in moves]
            for copy in copies:
                copy.start()
            arriving.append(copies)

    for b in range(BLOCKS):
        for f in range(SHARDS):
            x[b * RES:(b + 1) * RES, f * LANES:(f + 1) * LANES] = x_ref[b * SHARDS + f].astype(jnp.float32)

    for layer in range(LAYERS):
        base = layer * PART
        wide = x[...]
        scale = lax.rsqrt(jnp.mean(wide * wide, axis=-1, keepdims=True) + 1e-06)
        normed[...] = wide * scale * gain_ref[layer:layer + 1, :]
        shift = RES * 2**layer
        edge = jnp.zeros((shift, HALF), jnp.float32)
        for i in range(2):
            here = normed[:, half(i)]
            earlier = jnp.concatenate([edge, here[:ROWS - shift]], axis=0)
            later = jnp.concatenate([here[shift:], edge], axis=0)
            for t, rows in enumerate((earlier, here, later)):
                start = (3 * i + t) * HALF
                n[:, start:start + HALF] = rows.astype(jnp.bfloat16)

        def conv_column(k):
            if k == 0:
                return jnp.concatenate([mine[layer, t, half(i), :] for i in range(2) for t in range(3)], axis=0)
            return jnp.concatenate([w[2 * (k - 1) + i, base:base + 3 * HALF, :] for i in range(2)], axis=0)

        def mix_column(k):
            if k == 0:
                return jnp.concatenate([mine[layer, 3, half(i), :] for i in range(2)], axis=0)
            return jnp.concatenate([w[2 * (k - 1) + i, base + 3 * HALF:base + 4 * HALF, :] for i in range(2)], axis=0)

        def bias_row(k, start):
            rows = bias_ref[layer] if k == 0 else w[2 * (k - 1), base + 4 * HALF:base + PART, :]
            rows = rows.astype(jnp.float32)
            return rows[start:start + 1] + rows[start + 1:start + 2] + rows[start + 2:start + 3]

        for j in range(SHARDS // 2):
            pair = (2 * j, 2 * j + 1)
            for k in pair:
                for copy in arriving[layer * SHARDS + k]:
                    copy.wait()
            taps = jnp.concatenate([conv_column(k) for k in pair], axis=1)
            hidden = jnp.dot(n[...], taps, preferred_element_type=jnp.float32)
            hidden = hidden + jnp.concatenate([bias_row(k, 0) for k in pair], axis=1)
            done = (hidden * (1.0 + lax.erf(hidden * 0.7071067811865476)) * 0.5).astype(jnp.bfloat16)
            for h, k in enumerate(pair):
                act[:, home(k)] = done[:, h * LANES:(h + 1) * LANES]

        for i in range(2):
            mixing[:, i * HALF:(i + 1) * HALF] = act[:, half(i)]

        for j in range(SHARDS // 2):
            pair = (2 * j, 2 * j + 1)
            mixed = jnp.dot(mixing[...], jnp.concatenate([mix_column(k) for k in pair], axis=1), preferred_element_type=jnp.float32)
            mixed = mixed + jnp.concatenate([bias_row(k, 3) for k in pair], axis=1)
            for h, k in enumerate(pair):
                total = x[:, home(k)] + mixed[:, h * LANES:(h + 1) * LANES]
                if layer == LAYERS - 1:
                    f = homes[k]
                    for b in range(BLOCKS):
                        out_ref[b * SHARDS + f] = total[b * RES:(b + 1) * RES].astype(jnp.bfloat16)
                else:
                    x[:, home(k)] = total.astype(jnp.bfloat16).astype(jnp.float32)


def run_blocks(x, gain, bias, conv, mix, parts):
    vmem = pl.BlockSpec(memory_space=pltpu.VMEM)
    anywhere = pl.BlockSpec(memory_space=pl.ANY)
    return pl.pallas_call(
        blocks_kernel,
        out_shape=jax.ShapeDtypeStruct((BLOCKS * SHARDS, RES, LANES), jnp.bfloat16),
        in_specs=[vmem, vmem, vmem] + [anywhere] * (2 + len(parts)),
        out_specs=vmem,
        scratch_shapes=[
            pltpu.VMEM((len(parts), LAYERS * PART, LANES), jnp.bfloat16),
            pltpu.VMEM((LAYERS, 4, C, LANES), jnp.bfloat16),
            pltpu.VMEM((ROWS, C), jnp.float32),
            pltpu.VMEM((ROWS, C), jnp.float32),
            pltpu.VMEM((ROWS, 3 * C), jnp.bfloat16),
            pltpu.VMEM((ROWS, C), jnp.bfloat16),
            pltpu.VMEM((ROWS, C), jnp.bfloat16),
            pltpu.SemaphoreType.DMA((LAYERS, len(parts))),
            pltpu.SemaphoreType.DMA((LAYERS, 2)),
        ],
        compiler_params=pltpu.CompilerParams(vmem_limit_bytes=32 * 2**20),
        cost_estimate=pl.CostEstimate(flops=16 * ROWS * C * C, bytes_accessed=18 * 2**20, transcendentals=2 * ROWS * C),
        name="blocks",
    )(x, gain, bias, conv, mix, *parts)


def per_device(tokens, conv_weight, conv_bias, mix_weight, mix_bias, norm_gain):
    padded, own, bias = prepare(tokens, conv_weight, mix_weight, conv_bias, mix_bias)
    a = send(own, Z_SIDE)
    own_y = send(own, Y_SIDE)
    x = lax.all_to_all(padded.reshape(128, RES, LANES), AXES, split_axis=0, concat_axis=0, tiled=True)
    b = send(a, X_SIDE)
    e = send(a, Z_SIDE)
    a_y = send(a, Y_SIDE)
    a_y, e, b, x = lax.optimization_barrier((a_y, e, b, x))
    b_y = send(a_y, X_SIDE)
    e_y = send(e, Y_SIDE)
    mine = [a, b, e, own_y, a_y, b_y, e_y]
    swapped = [send(v, SWAP) for v in mine]
    parts = []
    for k, i in enumerate([1, 0, 2, 3, 5, 4, 6]):
        parts += [mine[k], swapped[i]]
    x = run_blocks(x, norm_gain, bias, conv_weight, mix_weight, parts)
    y = lax.all_to_all(x, AXES, split_axis=0, concat_axis=0, tiled=True)
    return y.reshape(128 * RES, LANES)[:tokens.shape[0]]


def solution(mesh):
    in_specs = (
        P("seq", "filt"),
        P(None, None, None, "filt"),
        P(None, "filt"),
        P(None, None, "filt"),
        P(None, "filt"),
        P(),
    )
    out_specs = P("seq", "filt")
    return jax.shard_map(
        per_device, mesh=mesh, in_specs=in_specs, out_specs=out_specs, check_vma=False
    )
```

```python
import functools

import jax
import jax.numpy as jnp
from jax import lax
from jax.experimental import pallas as pl
from jax.experimental.pallas import tpu as pltpu
from jax.sharding import PartitionSpec as P

LAYERS = 2
C = 1024
BLOCKS = 16
LANES = 128
SHARDS = 8
RES = 24
ROWS = BLOCKS * RES
EXTRA = 16
HALF = C // 2
PART = 4 * HALF + EXTRA
EARLY = 4
AXES = ("seq", "filt")


def coords(i):
    z, i = i % 4, i // 4
    yl, i = i % 2, i // 2
    c, i = i % 2, i // 2
    yh, x = i % 2, i // 2
    return x, yh * 2 + yl, z, c


def linear(x, y, z, c):
    x, y, z = x % 4, y % 4, z % 4
    return (((x * 2 + y // 2) * 2 + c) * 2 + y % 2) * 4 + z


def route(step):
    return [(i, linear(*step(*coords(i)))) for i in range(128)]


Z_SIDE = route(lambda x, y, z, c: (x, y, z + 1 - 2 * (c ^ x & 1), c))
Y_SIDE = route(lambda x, y, z, c: (x, y + 1 - 2 * c, z, c))
X_SIDE = route(lambda x, y, z, c: (x + 1 - 2 * c, y, z, c))
SWAP = route(lambda x, y, z, c: (x, y, z, 1 - c))


def place():
    seq, filt = lax.axis_index("seq"), lax.axis_index("filt")
    core, parity = seq & 1, (seq >> 2) & 1
    z, yl = filt & 3, filt >> 2
    side = 2 * (core ^ parity) - 1
    zs = [z, (z + side) & 3, (z - side) & 3, (z + 2) & 3]
    return core, [yl * 4 + v for v in zs] + [(1 - yl) * 4 + v for v in zs]


def send(block, path):
    return lax.ppermute(block, AXES, path)


def three_parts(v):
    hi = v.astype(jnp.bfloat16).astype(jnp.float32)
    mid = (v - hi).astype(jnp.bfloat16).astype(jnp.float32)
    lo = v - hi - mid
    return [hi, mid, lo]


def prepare_kernel(conv_ref, mix_ref, conv_bias_ref, mix_bias_ref, own_ref, bias_ref, own, sems, out_sems):
    core, _ = place()
    rows = pl.ds(pl.multiple_of(core * HALF, HALF), HALF)
    arriving, leaving = [], []
    for layer in range(LAYERS):
        for t in range(4):
            source = conv_ref.at[layer, t, rows] if t < 3 else mix_ref.at[layer, rows]
            spot = pl.ds(layer * PART + t * HALF, HALF)
            arriving.append((source, own.at[spot]))
            leaving.append((own.at[spot], own_ref.at[spot]))
    arriving = [pltpu.make_async_copy(a, b, sems.at[i]) for i, (a, b) in enumerate(arriving)]
    for copy in arriving:
        copy.start()
    for layer in range(LAYERS):
        lines = three_parts(conv_bias_ref[layer:layer + 1, :]) + three_parts(mix_bias_ref[layer:layer + 1, :])
        lines.append(jnp.zeros((EXTRA - 6, LANES), jnp.float32))
        block = jnp.concatenate(lines, axis=0).astype(jnp.bfloat16)
        spot = slice(layer * PART + 4 * HALF, (layer + 1) * PART)
        own[spot, :] = block
        bias_ref[layer] = block
        leaving.append((own.at[spot], own_ref.at[spot]))
    leaving = [pltpu.make_async_copy(a, b, out_sems.at[i]) for i, (a, b) in enumerate(leaving)]
    for copy in leaving[len(arriving):]:
        copy.start()
    for coming, going in zip(arriving, leaving):
        coming.wait()
        going.start()
    for copy in leaving:
        copy.wait()


def prepare(conv, mix, conv_bias, mix_bias):
    anywhere = pl.BlockSpec(memory_space=pl.ANY)
    vmem = pl.BlockSpec(memory_space=pltpu.VMEM)
    return pl.pallas_call(
        prepare_kernel,
        out_shape=[
            jax.ShapeDtypeStruct((LAYERS * PART, LANES), jnp.bfloat16),
            jax.ShapeDtypeStruct((LAYERS, EXTRA, LANES), jnp.bfloat16),
        ],
        in_specs=[anywhere, anywhere, vmem, vmem],
        out_specs=[anywhere, vmem],
        scratch_shapes=[
            pltpu.VMEM((LAYERS * PART, LANES), jnp.bfloat16),
            pltpu.SemaphoreType.DMA((4 * LAYERS,)),
            pltpu.SemaphoreType.DMA((5 * LAYERS,)),
        ],
        compiler_params=pltpu.CompilerParams(vmem_limit_bytes=60 * 2**20),
        cost_estimate=pl.CostEstimate(flops=0, bytes_accessed=4 * 2**20, transcendentals=0),
        name="prepare",
    )(conv, mix, conv_bias, mix_bias)


def sides(core):
    halves = (core, 1 - core)
    return [pl.ds(pl.multiple_of(v * HALF, HALF), HALF) for v in halves]


def home(shard):
    return pl.ds(pl.multiple_of(shard * LANES, LANES), LANES)


def normalize(layer, x, gain_ref, normed, n, halves):
    wide = x[...]
    scale = lax.rsqrt(jnp.mean(wide * wide, axis=-1, keepdims=True) + 1e-06)
    normed[...] = wide * scale * gain_ref[layer:layer + 1, :]
    shift = RES * 2**layer
    edge = jnp.zeros((shift, HALF), jnp.float32)
    for i in range(2):
        here = normed[:, halves[i]]
        earlier = jnp.concatenate([edge, here[:ROWS - shift]], axis=0)
        later = jnp.concatenate([here[shift:], edge], axis=0)
        for t, rows in enumerate((earlier, here, later)):
            start = (3 * i + t) * HALF
            n[:, start:start + HALF] = rows.astype(jnp.bfloat16)


def bias_row(rows, start):
    rows = rows.astype(jnp.float32)
    return rows[start:start + 1] + rows[start + 1:start + 2] + rows[start + 2:start + 3]


def convolve(n, columns, biases, act, homes):
    hidden = jnp.dot(n[...], jnp.concatenate(columns, axis=1), preferred_element_type=jnp.float32)
    hidden = hidden + jnp.concatenate([bias_row(v, 0) for v in biases], axis=1)
    done = (hidden * (1.0 + lax.erf(hidden * 0.7071067811865476)) * 0.5).astype(jnp.bfloat16)
    for h in range(2):
        act[:, home(homes[h])] = done[:, h * LANES:(h + 1) * LANES]


def head_kernel(x_ref, gain_ref, bias_ref, conv_ref, *rest):
    parts = rest[:2 * (EARLY - 1)]
    x, n, act, w, mine, normed, sems, mine_sem = rest[2 * (EARLY - 1):]
    core, homes = place()
    halves = sides(core)
    arriving = [[pltpu.make_async_copy(conv_ref.at[0], mine, mine_sem.at[0])]]
    for k in range(1, EARLY):
        copies = []
        for p in (2 * k - 2, 2 * k - 1):
            copies.append(pltpu.make_async_copy(parts[p].at[pl.ds(0, PART)], w.at[p], sems.at[p]))
        arriving.append(copies)
    for copies in arriving:
        for copy in copies:
            copy.start()
    for b in range(BLOCKS):
        for f in range(SHARDS):
            x[b * RES:(b + 1) * RES, f * LANES:(f + 1) * LANES] = x_ref[b * SHARDS + f].astype(jnp.float32)
    normalize(0, x, gain_ref, normed, n, halves)

    def column(k):
        if k == 0:
            return jnp.concatenate([mine[t, halves[i], :] for i in range(2) for t in range(3)], axis=0)
        return jnp.concatenate([w[2 * k - 2 + i, :3 * HALF, :] for i in range(2)], axis=0)

    for k in range(0, EARLY, 2):
        for copy in arriving[k] + arriving[k + 1]:
            copy.wait()
        biases = [bias_ref[0] if k == 0 else w[2 * k - 2, 4 * HALF:, :], w[2 * k, 4 * HALF:, :]]
        convolve(n, [column(k), column(k + 1)], biases, act, homes[k:k + 2])
    for k in range(EARLY, SHARDS):
        act[:, home(homes[k])] = jnp.zeros((ROWS, LANES), jnp.bfloat16)


def run_head(x, gain, bias, conv, parts):
    vmem = pl.BlockSpec(memory_space=pltpu.VMEM)
    anywhere = pl.BlockSpec(memory_space=pl.ANY)
    return pl.pallas_call(
        head_kernel,
        out_shape=[
            jax.ShapeDtypeStruct((ROWS, C), jnp.float32),
            jax.ShapeDtypeStruct((ROWS, 3 * C), jnp.bfloat16),
            jax.ShapeDtypeStruct((ROWS, C), jnp.bfloat16),
        ],
        in_specs=[vmem, vmem, vmem] + [anywhere] * (1 + len(parts)),
        out_specs=[vmem] * 3,
        scratch_shapes=[
            pltpu.VMEM((len(parts), PART, LANES), jnp.bfloat16),
            pltpu.VMEM((3, C, LANES), jnp.bfloat16),
            pltpu.VMEM((ROWS, C), jnp.float32),
            pltpu.SemaphoreType.DMA((len(parts),)),
            pltpu.SemaphoreType.DMA((1,)),
        ],
        compiler_params=pltpu.CompilerParams(vmem_limit_bytes=20 * 2**20),
        cost_estimate=pl.CostEstimate(flops=4 * ROWS * C * C, bytes_accessed=9 * 2**20, transcendentals=ROWS * C),
        name="head",
    )(x, gain, bias, conv, *parts)


def tail_kernel(x_ref, n_ref, act_ref, gain_ref, bias_ref, conv_ref, mix_ref, *rest):
    parts = rest[:2 * (SHARDS - 1)]
    out_ref, w, mine, x, normed, n, act, mixing, sems, late_sems, mine_sems = rest[2 * (SHARDS - 1):]
    core, homes = place()
    halves = sides(core)
    order = list(range(EARLY, SHARDS)) + list(range(EARLY))
    coming = {}
    for layer in range(LAYERS):
        for k in order if layer == 0 else range(SHARDS):
            if k == 0:
                copies = [pltpu.make_async_copy(mix_ref.at[layer], mine.at[layer, 3], mine_sems.at[layer, 1])]
                if layer > 0:
                    copies.append(pltpu.make_async_copy(conv_ref.at[layer], mine.at[layer, pl.ds(0, 3)], mine_sems.at[layer, 0]))
            else:
                rows = pl.ds(layer * PART, PART) if layer > 0 or k >= EARLY else pl.ds(3 * HALF, HALF + EXTRA)
                copies = []
                for p in (2 * k - 2, 2 * k - 1):
                    sem = (late_sems if layer > 0 else sems).at[p]
                    copies.append(pltpu.make_async_copy(parts[p].at[rows], w.at[p, rows], sem))
            for copy in copies:
                copy.start()
            coming[layer, k] = copies

    def arrived(layer, pair):
        for k in pair:
            for copy in coming.pop((layer, k), []):
                copy.wait()

    x[...] = x_ref[...]
    act[...] = act_ref[...]
    for layer in range(LAYERS):
        base = layer * PART

        def column(k, start, stop):
            if k == 0:
                return jnp.concatenate([mine[layer, t, halves[i], :] for i in range(2) for t in range(start, stop)], axis=0)
            spot = slice(base + start * HALF, base + stop * HALF)
            return jnp.concatenate([w[2 * k - 2 + i, spot, :] for i in range(2)], axis=0)

        def lines(k):
            return bias_ref[layer] if k == 0 else w[2 * k - 2, base + 4 * HALF:base + PART, :]

        if layer > 0:
            normalize(layer, x, gain_ref, normed, n, halves)
        for k in range(EARLY if layer == 0 else 0, SHARDS, 2):
            pair = (k, k + 1)
            arrived(layer, pair)
            convolve(n_ref if layer == 0 else n, [column(v, 0, 3) for v in pair], [lines(v) for v in pair], act, homes[k:k + 2])
        for i in range(2):
            mixing[:, i * HALF:(i + 1) * HALF] = act[:, halves[i]]
        for k in range(0, SHARDS, 2):
            pair = (k, k + 1)
            arrived(layer, pair)
            mixed = jnp.dot(mixing[...], jnp.concatenate([column(v, 3, 4) for v in pair], axis=1), preferred_element_type=jnp.float32)
            mixed = mixed + jnp.concatenate([bias_row(lines(v), 3) for v in pair], axis=1)
            for h, v in enumerate(pair):
                total = x[:, home(homes[v])] + mixed[:, h * LANES:(h + 1) * LANES]
                if layer == LAYERS - 1:
                    for b in range(BLOCKS):
                        out_ref[b * SHARDS + homes[v]] = total[b * RES:(b + 1) * RES].astype(jnp.bfloat16)
                else:
                    x[:, home(homes[v])] = total.astype(jnp.bfloat16).astype(jnp.float32)


def run_tail(x, n, act, gain, bias, conv, mix, parts):
    vmem = pl.BlockSpec(memory_space=pltpu.VMEM)
    anywhere = pl.BlockSpec(memory_space=pl.ANY)
    return pl.pallas_call(
        tail_kernel,
        out_shape=jax.ShapeDtypeStruct((BLOCKS * SHARDS, RES, LANES), jnp.bfloat16),
        in_specs=[vmem] * 5 + [anywhere] * (2 + len(parts)),
        out_specs=vmem,
        scratch_shapes=[
            pltpu.VMEM((len(parts), LAYERS * PART, LANES), jnp.bfloat16),
            pltpu.VMEM((LAYERS, 4, C, LANES), jnp.bfloat16),
            pltpu.VMEM((ROWS, C), jnp.float32),
            pltpu.VMEM((ROWS, C), jnp.float32),
            pltpu.VMEM((ROWS, 3 * C), jnp.bfloat16),
            pltpu.VMEM((ROWS, C), jnp.bfloat16),
            pltpu.VMEM((ROWS, C), jnp.bfloat16),
            pltpu.SemaphoreType.DMA((len(parts),)),
            pltpu.SemaphoreType.DMA((len(parts),)),
            pltpu.SemaphoreType.DMA((LAYERS, 2)),
        ],
        compiler_params=pltpu.CompilerParams(vmem_limit_bytes=30 * 2**20),
        cost_estimate=pl.CostEstimate(flops=12 * ROWS * C * C, bytes_accessed=14 * 2**20, transcendentals=ROWS * C),
        name="tail",
    )(x, n, act, gain, bias, conv, mix, *parts)


def per_device(tokens, conv_weight, conv_bias, mix_weight, mix_bias, norm_gain):
    own, bias = prepare(conv_weight, mix_weight, conv_bias, mix_bias)
    a = send(own, Z_SIDE)
    own_y = send(own, Y_SIDE)
    padded = jnp.pad(tokens, ((0, 128 * RES - tokens.shape[0]), (0, 0)))
    a, own_y, padded = lax.optimization_barrier((a, own_y, padded))
    x = lax.all_to_all(padded.reshape(128, RES, LANES), AXES, split_axis=0, concat_axis=0, tiled=True)
    b = send(a, X_SIDE)
    e = send(a, Z_SIDE)
    a_y = send(a, Y_SIDE)
    a_y, e, b, x = lax.optimization_barrier((a_y, e, b, x))
    b_y = send(a_y, X_SIDE)
    e_y = send(e, Y_SIDE)
    swapped = [send(v, SWAP) for v in (b, a, e)]
    early = [v for pair in zip((a, b, e), swapped) for v in pair]
    x, n, act = run_head(x, norm_gain, bias, conv_weight, early)
    b_y, e_y, act = lax.optimization_barrier((b_y, e_y, act))
    late = (own_y, a_y, b_y, e_y)
    swapped = [send(v, SWAP) for v in (own_y, b_y, a_y, e_y)]
    parts = early + [v for pair in zip(late, swapped) for v in pair]
    x = run_tail(x, n, act, norm_gain, bias, conv_weight, mix_weight, parts)
    y = lax.all_to_all(x, AXES, split_axis=0, concat_axis=0, tiled=True)
    return y.reshape(128 * RES, LANES)[:tokens.shape[0]]


def solution(mesh):
    in_specs = (
        P("seq", "filt"),
        P(None, None, None, "filt"),
        P(None, "filt"),
        P(None, None, "filt"),
        P(None, "filt"),
        P(),
    )
    out_specs = P("seq", "filt")
    return jax.shard_map(
        per_device, mesh=mesh, in_specs=in_specs, out_specs=out_specs, check_vma=False
    )
```

```python
import functools

import jax
import jax.numpy as jnp
from jax import lax
from jax.experimental import pallas as pl
from jax.experimental.pallas import tpu as pltpu
from jax.sharding import PartitionSpec as P

LAYERS = 2
C = 1024
BLOCKS = 16
LANES = 128
SHARDS = 8
RES = 24
ROWS = BLOCKS * RES
EXTRA = 16
HALF = C // 2
PART = 4 * HALF + EXTRA
EARLY = 4
AXES = ("seq", "filt")


def coords(i):
    z, i = i % 4, i // 4
    yl, i = i % 2, i // 2
    c, i = i % 2, i // 2
    yh, x = i % 2, i // 2
    return x, yh * 2 + yl, z, c


def linear(x, y, z, c):
    x, y, z = x % 4, y % 4, z % 4
    return (((x * 2 + y // 2) * 2 + c) * 2 + y % 2) * 4 + z


def route(step):
    return [(i, linear(*step(*coords(i)))) for i in range(128)]


Z_SIDE = route(lambda x, y, z, c: (x, y, z + 1 - 2 * (c ^ x & 1), c))
Y_SIDE = route(lambda x, y, z, c: (x, y + 1 - 2 * c, z, c))
X_SIDE = route(lambda x, y, z, c: (x + 1 - 2 * c, y, z, c))
SWAP = route(lambda x, y, z, c: (x, y, z, 1 - c))


def place():
    seq, filt = lax.axis_index("seq"), lax.axis_index("filt")
    core, parity = seq & 1, (seq >> 2) & 1
    z, yl = filt & 3, filt >> 2
    side = 2 * (core ^ parity) - 1
    zs = [z, (z + side) & 3, (z - side) & 3, (z + 2) & 3]
    return core, [yl * 4 + v for v in zs] + [(1 - yl) * 4 + v for v in zs]


def send(block, path):
    return lax.ppermute(block, AXES, path)


def three_parts(v):
    hi = v.astype(jnp.bfloat16).astype(jnp.float32)
    mid = (v - hi).astype(jnp.bfloat16).astype(jnp.float32)
    lo = v - hi - mid
    return [hi, mid, lo]


def prepare_kernel(conv_ref, mix_ref, conv_bias_ref, mix_bias_ref, own_ref, bias_ref, own, sems, out_sems):
    core, _ = place()
    rows = pl.ds(pl.multiple_of(core * HALF, HALF), HALF)
    arriving, leaving = [], []
    for layer in range(LAYERS):
        for t in range(4):
            source = conv_ref.at[layer, t, rows] if t < 3 else mix_ref.at[layer, rows]
            spot = pl.ds(layer * PART + t * HALF, HALF)
            arriving.append((source, own.at[spot]))
            leaving.append((own.at[spot], own_ref.at[spot]))
    arriving = [pltpu.make_async_copy(a, b, sems.at[i]) for i, (a, b) in enumerate(arriving)]
    for copy in arriving:
        copy.start()
    for layer in range(LAYERS):
        lines = three_parts(conv_bias_ref[layer:layer + 1, :]) + three_parts(mix_bias_ref[layer:layer + 1, :])
        lines.append(jnp.zeros((EXTRA - 6, LANES), jnp.float32))
        block = jnp.concatenate(lines, axis=0).astype(jnp.bfloat16)
        spot = slice(layer * PART + 4 * HALF, (layer + 1) * PART)
        own[spot, :] = block
        bias_ref[layer] = block
        leaving.append((own.at[spot], own_ref.at[spot]))
    leaving = [pltpu.make_async_copy(a, b, out_sems.at[i]) for i, (a, b) in enumerate(leaving)]
    for copy in leaving[len(arriving):]:
        copy.start()
    for coming, going in zip(arriving, leaving):
        coming.wait()
        going.start()
    for copy in leaving:
        copy.wait()


def prepare(conv, mix, conv_bias, mix_bias):
    anywhere = pl.BlockSpec(memory_space=pl.ANY)
    vmem = pl.BlockSpec(memory_space=pltpu.VMEM)
    return pl.pallas_call(
        prepare_kernel,
        out_shape=[
            jax.ShapeDtypeStruct((LAYERS * PART, LANES), jnp.bfloat16),
            jax.ShapeDtypeStruct((LAYERS, EXTRA, LANES), jnp.bfloat16),
        ],
        in_specs=[anywhere, anywhere, vmem, vmem],
        out_specs=[anywhere, vmem],
        scratch_shapes=[
            pltpu.VMEM((LAYERS * PART, LANES), jnp.bfloat16),
            pltpu.SemaphoreType.DMA((4 * LAYERS,)),
            pltpu.SemaphoreType.DMA((5 * LAYERS,)),
        ],
        compiler_params=pltpu.CompilerParams(vmem_limit_bytes=60 * 2**20),
        cost_estimate=pl.CostEstimate(flops=0, bytes_accessed=4 * 2**20, transcendentals=0),
        name="prepare",
    )(conv, mix, conv_bias, mix_bias)


def sides(core):
    halves = (core, 1 - core)
    return [pl.ds(pl.multiple_of(v * HALF, HALF), HALF) for v in halves]


def home(shard):
    return pl.ds(pl.multiple_of(shard * LANES, LANES), LANES)


def normalize(layer, x, gain_ref, normed, n, halves):
    wide = x[...]
    scale = lax.rsqrt(jnp.mean(wide * wide, axis=-1, keepdims=True) + 1e-06)
    normed[...] = wide * scale * gain_ref[layer:layer + 1, :]
    shift = RES * 2**layer
    edge = jnp.zeros((shift, HALF), jnp.float32)
    for i in range(2):
        here = normed[:, halves[i]]
        earlier = jnp.concatenate([edge, here[:ROWS - shift]], axis=0)
        later = jnp.concatenate([here[shift:], edge], axis=0)
        for t, rows in enumerate((earlier, here, later)):
            start = (3 * i + t) * HALF
            n[:, start:start + HALF] = rows.astype(jnp.bfloat16)


def bias_row(rows, start):
    rows = rows.astype(jnp.float32)
    return rows[start:start + 1] + rows[start + 1:start + 2] + rows[start + 2:start + 3]


def convolve(n, columns, biases, act, homes):
    hidden = jnp.dot(n[...], jnp.concatenate(columns, axis=1), preferred_element_type=jnp.float32)
    hidden = hidden + jnp.concatenate([bias_row(v, 0) for v in biases], axis=1)
    done = (hidden * (1.0 + lax.erf(hidden * 0.7071067811865476)) * 0.5).astype(jnp.bfloat16)
    for h in range(2):
        act[:, home(homes[h])] = done[:, h * LANES:(h + 1) * LANES]


def head_kernel(x_ref, gain_ref, bias_ref, conv_ref, *rest):
    parts = rest[:2 * (EARLY - 1)]
    x, n, act, w, mine, normed, sems, later_sems, mine_sem = rest[2 * (EARLY - 1):]
    core, homes = place()
    halves = sides(core)
    arriving = [[pltpu.make_async_copy(conv_ref.at[0], mine, mine_sem.at[0])]]
    for k in range(1, EARLY):
        copies = []
        for p in (2 * k - 2, 2 * k - 1):
            copies.append(pltpu.make_async_copy(parts[p].at[pl.ds(0, PART)], w.at[p, pl.ds(0, PART)], sems.at[p]))
        arriving.append(copies)
    rows = pl.ds(PART, (LAYERS - 1) * PART)
    later = [pltpu.make_async_copy(part.at[rows], w.at[p, rows], later_sems.at[p]) for p, part in enumerate(parts)]
    for copies in arriving + [later]:
        for copy in copies:
            copy.start()
    for b in range(BLOCKS):
        for f in range(SHARDS):
            x[b * RES:(b + 1) * RES, f * LANES:(f + 1) * LANES] = x_ref[b * SHARDS + f].astype(jnp.float32)
    normalize(0, x, gain_ref, normed, n, halves)

    def column(k):
        if k == 0:
            return jnp.concatenate([mine[t, halves[i], :] for i in range(2) for t in range(3)], axis=0)
        return jnp.concatenate([w[2 * k - 2 + i, :3 * HALF, :] for i in range(2)], axis=0)

    for k in range(0, EARLY, 2):
        for copy in arriving[k] + arriving[k + 1]:
            copy.wait()
        biases = [bias_ref[0] if k == 0 else w[2 * k - 2, 4 * HALF:PART, :], w[2 * k, 4 * HALF:PART, :]]
        convolve(n, [column(k), column(k + 1)], biases, act, homes[k:k + 2])
    for k in range(EARLY, SHARDS):
        act[:, home(homes[k])] = jnp.zeros((ROWS, LANES), jnp.bfloat16)
    for copy in later:
        copy.wait()


def run_head(x, gain, bias, conv, parts):
    vmem = pl.BlockSpec(memory_space=pltpu.VMEM)
    anywhere = pl.BlockSpec(memory_space=pl.ANY)
    return pl.pallas_call(
        head_kernel,
        out_shape=[
            jax.ShapeDtypeStruct((ROWS, C), jnp.float32),
            jax.ShapeDtypeStruct((ROWS, 3 * C), jnp.bfloat16),
            jax.ShapeDtypeStruct((ROWS, C), jnp.bfloat16),
            jax.ShapeDtypeStruct((len(parts), LAYERS * PART, LANES), jnp.bfloat16),
        ],
        in_specs=[vmem, vmem, vmem] + [anywhere] * (1 + len(parts)),
        out_specs=[vmem] * 4,
        scratch_shapes=[
            pltpu.VMEM((3, C, LANES), jnp.bfloat16),
            pltpu.VMEM((ROWS, C), jnp.float32),
            pltpu.SemaphoreType.DMA((len(parts),)),
            pltpu.SemaphoreType.DMA((len(parts),)),
            pltpu.SemaphoreType.DMA((1,)),
        ],
        compiler_params=pltpu.CompilerParams(vmem_limit_bytes=20 * 2**20),
        cost_estimate=pl.CostEstimate(flops=4 * ROWS * C * C, bytes_accessed=9 * 2**20, transcendentals=ROWS * C),
        name="head",
    )(x, gain, bias, conv, *parts)


def tail_kernel(x_ref, n_ref, act_ref, early_ref, gain_ref, bias_ref, conv_ref, mix_ref, *rest):
    parts = rest[:2 * (SHARDS - EARLY)]
    out_ref, w, mine, x, normed, n, act, mixing, sems, late_sems, mine_sems = rest[2 * (SHARDS - EARLY):]
    core, homes = place()
    halves = sides(core)
    order = list(range(EARLY, SHARDS)) + list(range(EARLY))
    coming = {}
    for layer in range(LAYERS):
        for k in order if layer == 0 else range(SHARDS):
            if k == 0:
                copies = [pltpu.make_async_copy(mix_ref.at[layer], mine.at[layer, 3], mine_sems.at[layer, 1])]
                if layer > 0:
                    copies.append(pltpu.make_async_copy(conv_ref.at[layer], mine.at[layer, pl.ds(0, 3)], mine_sems.at[layer, 0]))
            elif k < EARLY:
                continue
            else:
                rows = pl.ds(layer * PART, PART)
                copies = []
                for p in (2 * (k - EARLY), 2 * (k - EARLY) + 1):
                    sem = (late_sems if layer > 0 else sems).at[p]
                    copies.append(pltpu.make_async_copy(parts[p].at[rows], w.at[p, rows], sem))
            for copy in copies:
                copy.start()
            coming[layer, k] = copies

    def arrived(layer, pair):
        for k in pair:
            for copy in coming.pop((layer, k), []):
                copy.wait()

    def block(k, i, spot):
        return early_ref[2 * k - 2 + i, spot, :] if k < EARLY else w[2 * (k - EARLY) + i, spot, :]

    x[...] = x_ref[...]
    act[...] = act_ref[...]
    for layer in range(LAYERS):
        base = layer * PART

        def column(k, start, stop):
            if k == 0:
                return jnp.concatenate([mine[layer, t, halves[i], :] for i in range(2) for t in range(start, stop)], axis=0)
            spot = slice(base + start * HALF, base + stop * HALF)
            return jnp.concatenate([block(k, i, spot) for i in range(2)], axis=0)

        def lines(k):
            return bias_ref[layer] if k == 0 else block(k, 0, slice(base + 4 * HALF, base + PART))

        if layer > 0:
            normalize(layer, x, gain_ref, normed, n, halves)
        for k in range(EARLY if layer == 0 else 0, SHARDS, 2):
            pair = (k, k + 1)
            arrived(layer, pair)
            convolve(n_ref if layer == 0 else n, [column(v, 0, 3) for v in pair], [lines(v) for v in pair], act, homes[k:k + 2])
        for i in range(2):
            mixing[:, i * HALF:(i + 1) * HALF] = act[:, halves[i]]
        for k in range(0, SHARDS, 2):
            pair = (k, k + 1)
            arrived(layer, pair)
            mixed = jnp.dot(mixing[...], jnp.concatenate([column(v, 3, 4) for v in pair], axis=1), preferred_element_type=jnp.float32)
            mixed = mixed + jnp.concatenate([bias_row(lines(v), 3) for v in pair], axis=1)
            for h, v in enumerate(pair):
                total = x[:, home(homes[v])] + mixed[:, h * LANES:(h + 1) * LANES]
                if layer == LAYERS - 1:
                    for b in range(BLOCKS):
                        out_ref[b * SHARDS + homes[v]] = total[b * RES:(b + 1) * RES].astype(jnp.bfloat16)
                else:
                    x[:, home(homes[v])] = total.astype(jnp.bfloat16).astype(jnp.float32)


def run_tail(x, n, act, early, gain, bias, conv, mix, parts):
    vmem = pl.BlockSpec(memory_space=pltpu.VMEM)
    anywhere = pl.BlockSpec(memory_space=pl.ANY)
    return pl.pallas_call(
        tail_kernel,
        out_shape=jax.ShapeDtypeStruct((BLOCKS * SHARDS, RES, LANES), jnp.bfloat16),
        in_specs=[vmem] * 6 + [anywhere] * (2 + len(parts)),
        out_specs=vmem,
        scratch_shapes=[
            pltpu.VMEM((len(parts), LAYERS * PART, LANES), jnp.bfloat16),
            pltpu.VMEM((LAYERS, 4, C, LANES), jnp.bfloat16),
            pltpu.VMEM((ROWS, C), jnp.float32),
            pltpu.VMEM((ROWS, C), jnp.float32),
            pltpu.VMEM((ROWS, 3 * C), jnp.bfloat16),
            pltpu.VMEM((ROWS, C), jnp.bfloat16),
            pltpu.VMEM((ROWS, C), jnp.bfloat16),
            pltpu.SemaphoreType.DMA((len(parts),)),
            pltpu.SemaphoreType.DMA((len(parts),)),
            pltpu.SemaphoreType.DMA((LAYERS, 2)),
        ],
        compiler_params=pltpu.CompilerParams(vmem_limit_bytes=24 * 2**20),
        cost_estimate=pl.CostEstimate(flops=12 * ROWS * C * C, bytes_accessed=14 * 2**20, transcendentals=ROWS * C),
        name="tail",
    )(x, n, act, early, gain, bias, conv, mix, *parts)


def per_device(tokens, conv_weight, conv_bias, mix_weight, mix_bias, norm_gain):
    own, bias = prepare(conv_weight, mix_weight, conv_bias, mix_bias)
    a = send(own, Z_SIDE)
    own_y = send(own, Y_SIDE)
    padded = jnp.pad(tokens, ((0, 128 * RES - tokens.shape[0]), (0, 0)))
    a, own_y, padded = lax.optimization_barrier((a, own_y, padded))
    x = lax.all_to_all(padded.reshape(128, RES, LANES), AXES, split_axis=0, concat_axis=0, tiled=True)
    b = send(a, X_SIDE)
    e = send(a, Z_SIDE)
    a_y = send(a, Y_SIDE)
    a_y, e, b, x = lax.optimization_barrier((a_y, e, b, x))
    b_y = send(a_y, X_SIDE)
    e_y = send(e, Y_SIDE)
    swapped = [send(v, SWAP) for v in (b, a, e)]
    early = [v for pair in zip((a, b, e), swapped) for v in pair]
    x, n, act, kept = run_head(x, norm_gain, bias, conv_weight, early)
    b_y, e_y, act = lax.optimization_barrier((b_y, e_y, act))
    late = (own_y, a_y, b_y, e_y)
    swapped = [send(v, SWAP) for v in (own_y, b_y, a_y, e_y)]
    parts = [v for pair in zip(late, swapped) for v in pair]
    x = run_tail(x, n, act, kept, norm_gain, bias, conv_weight, mix_weight, parts)
    y = lax.all_to_all(x, AXES, split_axis=0, concat_axis=0, tiled=True)
    return y.reshape(128 * RES, LANES)[:tokens.shape[0]]


def solution(mesh):
    in_specs = (
        P("seq", "filt"),
        P(None, None, None, "filt"),
        P(None, "filt"),
        P(None, None, "filt"),
        P(None, "filt"),
        P(),
    )
    out_specs = P("seq", "filt")
    return jax.shard_map(
        per_device, mesh=mesh, in_specs=in_specs, out_specs=out_specs, check_vma=False
    )
```

```python
import functools

import jax
import jax.numpy as jnp
from jax import lax
from jax.experimental import pallas as pl
from jax.experimental.pallas import tpu as pltpu
from jax.sharding import PartitionSpec as P

LAYERS = 2
C = 1024
BLOCKS = 16
LANES = 128
SHARDS = 8
RES = 24
ROWS = BLOCKS * RES
EXTRA = 16
HALF = C // 2
PART = 4 * HALF + EXTRA
EARLY = 4
AXES = ("seq", "filt")


def coords(i):
    z, i = i % 4, i // 4
    yl, i = i % 2, i // 2
    c, i = i % 2, i // 2
    yh, x = i % 2, i // 2
    return x, yh * 2 + yl, z, c


def linear(x, y, z, c):
    x, y, z = x % 4, y % 4, z % 4
    return (((x * 2 + y // 2) * 2 + c) * 2 + y % 2) * 4 + z


def route(step):
    return [(i, linear(*step(*coords(i)))) for i in range(128)]


Z_SIDE = route(lambda x, y, z, c: (x, y, z + 1 - 2 * (c ^ x & 1), c))
Y_SIDE = route(lambda x, y, z, c: (x, y + 1 - 2 * c, z, c))
X_SIDE = route(lambda x, y, z, c: (x + 1 - 2 * c, y, z, c))
SWAP = route(lambda x, y, z, c: (x, y, z, 1 - c))


def place():
    seq, filt = lax.axis_index("seq"), lax.axis_index("filt")
    core, parity = seq & 1, (seq >> 2) & 1
    z, yl = filt & 3, filt >> 2
    side = 2 * (core ^ parity) - 1
    zs = [z, (z + side) & 3, (z - side) & 3, (z + 2) & 3]
    return core, [yl * 4 + v for v in zs] + [(1 - yl) * 4 + v for v in zs]


def send(block, path):
    return lax.ppermute(block, AXES, path)


def three_parts(v):
    hi = v.astype(jnp.bfloat16).astype(jnp.float32)
    mid = (v - hi).astype(jnp.bfloat16).astype(jnp.float32)
    lo = v - hi - mid
    return [hi, mid, lo]


def prepare_kernel(conv_ref, mix_ref, conv_bias_ref, mix_bias_ref, own_ref, bias_ref, own, sems, out_sems):
    core, _ = place()
    rows = pl.ds(pl.multiple_of(core * HALF, HALF), HALF)
    arriving, leaving = [], []
    for layer in range(LAYERS):
        for t in range(4):
            source = conv_ref.at[layer, t, rows] if t < 3 else mix_ref.at[layer, rows]
            spot = pl.ds(layer * PART + t * HALF, HALF)
            arriving.append((source, own.at[spot]))
            leaving.append((own.at[spot], own_ref.at[spot]))
    arriving = [pltpu.make_async_copy(a, b, sems.at[i]) for i, (a, b) in enumerate(arriving)]
    for copy in arriving:
        copy.start()
    for layer in range(LAYERS):
        lines = three_parts(conv_bias_ref[layer:layer + 1, :]) + three_parts(mix_bias_ref[layer:layer + 1, :])
        lines.append(jnp.zeros((EXTRA - 6, LANES), jnp.float32))
        block = jnp.concatenate(lines, axis=0).astype(jnp.bfloat16)
        spot = slice(layer * PART + 4 * HALF, (layer + 1) * PART)
        own[spot, :] = block
        bias_ref[layer] = block
        leaving.append((own.at[spot], own_ref.at[spot]))
    leaving = [pltpu.make_async_copy(a, b, out_sems.at[i]) for i, (a, b) in enumerate(leaving)]
    for copy in leaving[len(arriving):]:
        copy.start()
    for coming, going in zip(arriving, leaving):
        coming.wait()
        going.start()
    for copy in leaving:
        copy.wait()


def prepare(conv, mix, conv_bias, mix_bias):
    anywhere = pl.BlockSpec(memory_space=pl.ANY)
    vmem = pl.BlockSpec(memory_space=pltpu.VMEM)
    return pl.pallas_call(
        prepare_kernel,
        out_shape=[
            jax.ShapeDtypeStruct((LAYERS * PART, LANES), jnp.bfloat16),
            jax.ShapeDtypeStruct((LAYERS, EXTRA, LANES), jnp.bfloat16),
        ],
        in_specs=[anywhere, anywhere, vmem, vmem],
        out_specs=[anywhere, vmem],
        scratch_shapes=[
            pltpu.VMEM((LAYERS * PART, LANES), jnp.bfloat16),
            pltpu.SemaphoreType.DMA((4 * LAYERS,)),
            pltpu.SemaphoreType.DMA((5 * LAYERS,)),
        ],
        compiler_params=pltpu.CompilerParams(vmem_limit_bytes=60 * 2**20),
        cost_estimate=pl.CostEstimate(flops=0, bytes_accessed=4 * 2**20, transcendentals=0),
        name="prepare",
    )(conv, mix, conv_bias, mix_bias)


def sides(core):
    halves = (core, 1 - core)
    return [pl.ds(pl.multiple_of(v * HALF, HALF), HALF) for v in halves]


def home(shard):
    return pl.ds(pl.multiple_of(shard * LANES, LANES), LANES)


def normalize(layer, x, gain_ref, normed, n, halves):
    wide = x[...]
    scale = lax.rsqrt(jnp.mean(wide * wide, axis=-1, keepdims=True) + 1e-06)
    normed[...] = wide * scale * gain_ref[layer:layer + 1, :]
    shift = RES * 2**layer
    edge = jnp.zeros((shift, HALF), jnp.float32)
    for i in range(2):
        here = normed[:, halves[i]]
        earlier = jnp.concatenate([edge, here[:ROWS - shift]], axis=0)
        later = jnp.concatenate([here[shift:], edge], axis=0)
        for t, rows in enumerate((earlier, here, later)):
            start = (3 * i + t) * HALF
            n[:, start:start + HALF] = rows.astype(jnp.bfloat16)


def bias_row(rows, start):
    rows = rows.astype(jnp.float32)
    return rows[start:start + 1] + rows[start + 1:start + 2] + rows[start + 2:start + 3]


def convolve(n, columns, biases, act, homes):
    hidden = jnp.dot(n[...], jnp.concatenate(columns, axis=1), preferred_element_type=jnp.float32)
    hidden = hidden + jnp.concatenate([bias_row(v, 0) for v in biases], axis=1)
    done = (hidden * (1.0 + lax.erf(hidden * 0.7071067811865476)) * 0.5).astype(jnp.bfloat16)
    for h in range(2):
        act[:, home(homes[h])] = done[:, h * LANES:(h + 1) * LANES]


def head_kernel(x_ref, gain_ref, bias_ref, conv_ref, *rest):
    parts = rest[:2 * (EARLY - 1)]
    x, n, act, w, mine, normed, sems, later_sems, mine_sem = rest[2 * (EARLY - 1):]
    core, homes = place()
    halves = sides(core)
    arriving = [[pltpu.make_async_copy(conv_ref.at[0], mine, mine_sem.at[0])]]
    for k in range(1, EARLY):
        copies = []
        for p in (2 * k - 2, 2 * k - 1):
            copies.append(pltpu.make_async_copy(parts[p].at[pl.ds(0, PART)], w.at[p, pl.ds(0, PART)], sems.at[p]))
        arriving.append(copies)
    rows = pl.ds(PART, (LAYERS - 1) * PART)
    later = [pltpu.make_async_copy(part.at[rows], w.at[p, rows], later_sems.at[p]) for p, part in enumerate(parts)]
    for copies in arriving + [later]:
        for copy in copies:
            copy.start()
    for b in range(BLOCKS):
        for f in range(SHARDS):
            x[b * RES:(b + 1) * RES, f * LANES:(f + 1) * LANES] = x_ref[b * SHARDS + f].astype(jnp.float32)
    normalize(0, x, gain_ref, normed, n, halves)

    def column(k):
        if k == 0:
            return jnp.concatenate([mine[t, halves[i], :] for i in range(2) for t in range(3)], axis=0)
        return jnp.concatenate([w[2 * k - 2 + i, :3 * HALF, :] for i in range(2)], axis=0)

    for k in range(0, EARLY, 2):
        for copy in arriving[k] + arriving[k + 1]:
            copy.wait()
        biases = [bias_ref[0] if k == 0 else w[2 * k - 2, 4 * HALF:PART, :], w[2 * k, 4 * HALF:PART, :]]
        convolve(n, [column(k), column(k + 1)], biases, act, homes[k:k + 2])
    for k in range(EARLY, SHARDS):
        act[:, home(homes[k])] = jnp.zeros((ROWS, LANES), jnp.bfloat16)
    for copy in later:
        copy.wait()


def run_head(x, gain, bias, conv, parts):
    vmem = pl.BlockSpec(memory_space=pltpu.VMEM)
    anywhere = pl.BlockSpec(memory_space=pl.ANY)
    return pl.pallas_call(
        head_kernel,
        out_shape=[
            jax.ShapeDtypeStruct((ROWS, C), jnp.float32),
            jax.ShapeDtypeStruct((ROWS, 3 * C), jnp.bfloat16),
            jax.ShapeDtypeStruct((ROWS, C), jnp.bfloat16),
            jax.ShapeDtypeStruct((len(parts), LAYERS * PART, LANES), jnp.bfloat16),
        ],
        in_specs=[vmem, vmem, vmem] + [anywhere] * (1 + len(parts)),
        out_specs=[vmem] * 4,
        scratch_shapes=[
            pltpu.VMEM((3, C, LANES), jnp.bfloat16),
            pltpu.VMEM((ROWS, C), jnp.float32),
            pltpu.SemaphoreType.DMA((len(parts),)),
            pltpu.SemaphoreType.DMA((len(parts),)),
            pltpu.SemaphoreType.DMA((1,)),
        ],
        compiler_params=pltpu.CompilerParams(vmem_limit_bytes=20 * 2**20),
        cost_estimate=pl.CostEstimate(flops=4 * ROWS * C * C, bytes_accessed=9 * 2**20, transcendentals=ROWS * C),
        name="head",
    )(x, gain, bias, conv, *parts)


def tail_kernel(x_ref, n_ref, act_ref, early_ref, gain_ref, bias_ref, conv_ref, mix_ref, *rest):
    parts = rest[:2 * (SHARDS - EARLY)]
    out_ref, w, mine, x, normed, n, act, mixing, sems, late_sems, mine_sems = rest[2 * (SHARDS - EARLY):]
    core, homes = place()
    halves = sides(core)
    order = list(range(EARLY, SHARDS)) + list(range(EARLY))
    coming = {}
    for layer in range(LAYERS):
        for k in order if layer == 0 else range(SHARDS):
            if k == 0:
                copies = [pltpu.make_async_copy(mix_ref.at[layer], mine.at[layer, 3], mine_sems.at[layer, 1])]
                if layer > 0:
                    copies.append(pltpu.make_async_copy(conv_ref.at[layer], mine.at[layer, pl.ds(0, 3)], mine_sems.at[layer, 0]))
            elif k < EARLY:
                continue
            else:
                rows = pl.ds(layer * PART, PART)
                copies = []
                for p in (2 * (k - EARLY), 2 * (k - EARLY) + 1):
                    sem = (late_sems if layer > 0 else sems).at[p]
                    copies.append(pltpu.make_async_copy(parts[p].at[rows], w.at[p, rows], sem))
            for copy in copies:
                copy.start()
            coming[layer, k] = copies

    def arrived(layer, pair):
        for k in pair:
            for copy in coming.pop((layer, k), []):
                copy.wait()

    def block(k, i, spot):
        return early_ref[2 * k - 2 + i, spot, :] if k < EARLY else w[2 * (k - EARLY) + i, spot, :]

    x[...] = x_ref[...]
    act[...] = act_ref[...]
    for layer in range(LAYERS):
        base = layer * PART

        def column(k, start, stop):
            if k == 0:
                return jnp.concatenate([mine[layer, t, halves[i], :] for i in range(2) for t in range(start, stop)], axis=0)
            spot = slice(base + start * HALF, base + stop * HALF)
            return jnp.concatenate([block(k, i, spot) for i in range(2)], axis=0)

        def lines(k):
            return bias_ref[layer] if k == 0 else block(k, 0, slice(base + 4 * HALF, base + PART))

        if layer > 0:
            normalize(layer, x, gain_ref, normed, n, halves)
        for k in range(EARLY if layer == 0 else 0, SHARDS, 2):
            pair = (k, k + 1)
            arrived(layer, pair)
            convolve(n_ref if layer == 0 else n, [column(v, 0, 3) for v in pair], [lines(v) for v in pair], act, homes[k:k + 2])
        for i in range(2):
            mixing[:, i * HALF:(i + 1) * HALF] = act[:, halves[i]]
        for k in range(0, SHARDS, 2):
            pair = (k, k + 1)
            arrived(layer, pair)
            mixed = jnp.dot(mixing[...], jnp.concatenate([column(v, 3, 4) for v in pair], axis=1), preferred_element_type=jnp.float32)
            mixed = mixed + jnp.concatenate([bias_row(lines(v), 3) for v in pair], axis=1)
            for h, v in enumerate(pair):
                total = x[:, home(homes[v])] + mixed[:, h * LANES:(h + 1) * LANES]
                if layer == LAYERS - 1:
                    for b in range(BLOCKS):
                        out_ref[b * SHARDS + homes[v]] = total[b * RES:(b + 1) * RES].astype(jnp.bfloat16)
                else:
                    x[:, home(homes[v])] = total.astype(jnp.bfloat16).astype(jnp.float32)


def run_tail(x, n, act, early, gain, bias, conv, mix, parts):
    vmem = pl.BlockSpec(memory_space=pltpu.VMEM)
    anywhere = pl.BlockSpec(memory_space=pl.ANY)
    return pl.pallas_call(
        tail_kernel,
        out_shape=jax.ShapeDtypeStruct((BLOCKS * SHARDS, RES, LANES), jnp.bfloat16),
        in_specs=[vmem] * 6 + [anywhere] * (2 + len(parts)),
        out_specs=vmem,
        scratch_shapes=[
            pltpu.VMEM((len(parts), LAYERS * PART, LANES), jnp.bfloat16),
            pltpu.VMEM((LAYERS, 4, C, LANES), jnp.bfloat16),
            pltpu.VMEM((ROWS, C), jnp.float32),
            pltpu.VMEM((ROWS, C), jnp.float32),
            pltpu.VMEM((ROWS, 3 * C), jnp.bfloat16),
            pltpu.VMEM((ROWS, C), jnp.bfloat16),
            pltpu.VMEM((ROWS, C), jnp.bfloat16),
            pltpu.SemaphoreType.DMA((len(parts),)),
            pltpu.SemaphoreType.DMA((len(parts),)),
            pltpu.SemaphoreType.DMA((LAYERS, 2)),
        ],
        compiler_params=pltpu.CompilerParams(vmem_limit_bytes=24 * 2**20),
        cost_estimate=pl.CostEstimate(flops=12 * ROWS * C * C, bytes_accessed=14 * 2**20, transcendentals=ROWS * C),
        name="tail",
    )(x, n, act, early, gain, bias, conv, mix, *parts)


def per_device(tokens, conv_weight, conv_bias, mix_weight, mix_bias, norm_gain):
    own, bias = prepare(conv_weight, mix_weight, conv_bias, mix_bias)
    a = send(own, Z_SIDE)
    own_y = send(own, Y_SIDE)
    padded = jnp.pad(tokens, ((0, 128 * RES - tokens.shape[0]), (0, 0)))
    x = lax.all_to_all(padded.reshape(128, RES, LANES), AXES, split_axis=0, concat_axis=0, tiled=True)
    a, own_y, x = lax.optimization_barrier((a, own_y, x))
    b = send(a, X_SIDE)
    e = send(a, Z_SIDE)
    a_y = send(a, Y_SIDE)
    a_y, e, b = lax.optimization_barrier((a_y, e, b))
    b_y = send(a_y, X_SIDE)
    e_y = send(e, Y_SIDE)
    swapped = [send(v, SWAP) for v in (b, a, e)]
    early = [v for pair in zip((a, b, e), swapped) for v in pair]
    x, n, act, kept = run_head(x, norm_gain, bias, conv_weight, early)
    b_y, e_y, act = lax.optimization_barrier((b_y, e_y, act))
    late = (own_y, a_y, b_y, e_y)
    swapped = [send(v, SWAP) for v in (own_y, b_y, a_y, e_y)]
    parts = [v for pair in zip(late, swapped) for v in pair]
    x = run_tail(x, n, act, kept, norm_gain, bias, conv_weight, mix_weight, parts)
    y = lax.all_to_all(x, AXES, split_axis=0, concat_axis=0, tiled=True)
    return y.reshape(128 * RES, LANES)[:tokens.shape[0]]


def solution(mesh):
    in_specs = (
        P("seq", "filt"),
        P(None, None, None, "filt"),
        P(None, "filt"),
        P(None, None, "filt"),
        P(None, "filt"),
        P(),
    )
    out_specs = P("seq", "filt")
    return jax.shard_map(
        per_device, mesh=mesh, in_specs=in_specs, out_specs=out_specs, check_vma=False
    )
```
